128 devices in a mesh: sec: 2 (over core), tile: 64 (over z, y, x).
Axes of the slice: x: 4, y: 4, z: 4, core: 2. Of those that a mesh axis runs over, the one named last changes fastest.
Arguments:
- adjoint_state: bfloat16 [2, 75, 2359296], P('sec', None, 'tile'), may hold values from -6 to 6
- tangent_coef: bfloat16 [2, 75, 2359296], P('sec', None, 'tile'), may hold values from 0.5 to 1.5
- column_ops: bfloat16 [2, 16, 75, 75], P('sec')
- surf_read: bfloat16 [2, 4, 75], P('sec'), may hold values from -0.75 to 0.75
- surf_write: float32 [2, 75, 4], P('sec'), may hold values from -3 to 3
- remap_weights: bfloat16 [64, 64, 16, 4096], P('tile')
- pair_atmos: int32 [64, 64, 16], P('tile'), may hold values from 0 to 575
- pair_ocean: int32 [64, 64, 16], P('tile'), may hold values from 0 to 36863, as said below
- list_len: int32 [64, 64], P('tile'), may hold values from 0 to 16, as said below
- ocean_owned: int32 [64, 576], P('tile'), may hold values from 0 to 36863, as said below
Outputs:
- adjoint_out: bfloat16 [2, 75, 2359296], P('sec', None, 'tile')
The draws below stay inside these ranges and needn't reach their ends.
Inputs may be any that keep to these rules, and one draw needn't show every extreme that they name: pair_ocean[t, d, c] is one of the blocks in row d of ocean_owned. Every global ocean block stands exactly once in ocean_owned. Slots c >= list_len[t, d] are empty; in every draw some ocean tile receives a full list of 16 pairs from every atmosphere tile.
All inputs are finite; a program needn't handle non-finite values.
Results may differ from the reference program's by a relative error of at most 0.012.
Values may be sent and summed in bfloat16 or wider, within the bound.
No kernel may reach another device: no remote copies, remote signals or barrier semaphores. Data moves between devices by JAX's collectives and lax.ppermute only.
A program may use at most 128 MiB of HBM per device.

```python
import jax
import jax.numpy as jnp
from jax import lax

LEV = 75
NF = 4
BLK = 64
CAP = 16
NSTEP = 16
CELL_DEV = 36864
TILES = 64
BLOCKS_DEV = 576
CELLS = 2359296


def ownership(key):
    order = jax.random.permutation(jax.random.fold_in(key, 11), TILES * BLOCKS_DEV)
    return order.astype(jnp.int32).reshape(TILES, BLOCKS_DEV)


def draw_ocean_owned(key, part):
    return ownership(key)


def draw_pair_ocean(key, part):
    owned = ownership(key)
    chosen = jax.random.randint(jax.random.fold_in(key, 12), (TILES, TILES, CAP), 0, BLOCKS_DEV)
    tile_index = jnp.arange(TILES, dtype=jnp.int32)[None, :, None]
    return owned[tile_index, chosen].astype(jnp.int32)


def draw_list_len(key, part):
    lengths = jax.random.randint(jax.random.fold_in(key, 21), (TILES, TILES), 0, CAP + 1)
    full_tile = jax.random.randint(jax.random.fold_in(key, 22), (), 0, TILES)
    tile_index = jnp.arange(TILES, dtype=jnp.int32)
    return jnp.where(tile_index[None, :] == full_tile, CAP, lengths).astype(jnp.int32)


def draw_column_ops(key, part):
    noise_part = jax.random.normal(jax.random.fold_in(key, 31), (2, NSTEP, LEV, LEV), jnp.float32)
    level_index = jnp.arange(LEV)
    identity = (level_index[:, None] == level_index[None, :]).astype(jnp.float32)
    return (0.9 * identity + 0.35 * LEV ** (-0.5) * noise_part).astype(jnp.bfloat16)


def draw_remap_weights(key, part):
    spread_part = jax.random.uniform(jax.random.fold_in(key, 41), (TILES, TILES, CAP, BLK, BLK), jnp.float32, 0.0, 2.0 / BLK)
    cell_index = jnp.arange(BLK)
    identity = (cell_index[:, None] == cell_index[None, :]).astype(jnp.float32)
    weights = 0.5 * identity + spread_part * (1.0 - identity)
    return weights.reshape(TILES, TILES, CAP, BLK * BLK).astype(jnp.bfloat16)


def plant(drawn, own_key, least, top_value):
    longest = drawn.shape.index(max(drawn.shape))
    spots = []
    for shift in (0, 1):
        where = [jax.random.randint(jax.random.fold_in(own_key, axis), (), 0, length) for axis, length in enumerate(drawn.shape)]
        where[longest] = (where[longest] + shift) % drawn.shape[longest]
        spots.append(tuple(where))
    return drawn.at[spots[0]].set(least).at[spots[1]].set(top_value)


def levels(own_key, extent, shards, least, top_value):
    loudness = 1.0
    for position, shards_of in shards:
        heights = jax.random.uniform(jax.random.fold_in(jax.random.fold_in(own_key, 6), position), (shards_of,), jnp.float32, least / len(shards), top_value / len(shards))
        loudness = loudness * jnp.repeat(jnp.exp(heights), extent[position] // shards_of).reshape((-1,) + (1,) * (len(extent) - 1 - position))
    return loudness


def noise(key, extent, deviation, limit, shards=(), kind=jnp.bfloat16):
    entries = jax.random.normal(key, extent, jnp.float32) * deviation
    if len(shards) > 0:
        entries = levels(key, extent, shards, -0.22, 0.18) * entries
    return jnp.clip(entries, min=-limit, max=limit).astype(kind)


def setup_inputs(seed: int = 0) -> dict:
    seeds = jax.random.split(jax.random.key(seed), 11)
    adjoint_state = noise(seeds[0], (2, LEV, CELLS), 1.0, 6.0, ((0, 2), (2, 64)))
    tangent_coef = jnp.clip(1.0 + 0.1 * jax.random.normal(seeds[1], (2, LEV, CELLS), jnp.float32), 0.5, 1.5).astype(jnp.bfloat16)
    column_ops = draw_column_ops(jax.random.fold_in(seeds[10], 71), 0)
    surf_read = noise(seeds[3], (2, NF, LEV), LEV ** -0.5, 0.75, ((0, 2),))
    surf_write = noise(seeds[4], (2, LEV, NF), NF ** -0.5, 3.0, ((0, 2),), jnp.float32)
    remap_weights = draw_remap_weights(jax.random.fold_in(seeds[10], 71), 0)
    pair_atmos = plant(jax.random.randint(seeds[6], (TILES, TILES, CAP), 0, BLOCKS_DEV), jax.random.fold_in(seeds[6], 1), 0, BLOCKS_DEV - 1).astype(jnp.int32)
    pair_ocean = draw_pair_ocean(jax.random.fold_in(seeds[10], 71), 0)
    list_len = draw_list_len(jax.random.fold_in(seeds[10], 71), 0)
    ocean_owned = draw_ocean_owned(jax.random.fold_in(seeds[10], 71), 0)
    return dict(adjoint_state=adjoint_state, tangent_coef=tangent_coef, column_ops=column_ops, surf_read=surf_read, surf_write=surf_write, remap_weights=remap_weights, pair_atmos=pair_atmos, pair_ocean=pair_ocean, list_len=list_len, ocean_owned=ocean_owned)


def sweep_section(state_part, coef_part, ops_part):
    columns = state_part.reshape(LEV, TILES, CELL_DEV).transpose(1, 0, 2)
    factors = coef_part.reshape(LEV, TILES, CELL_DEV).transpose(1, 0, 2)

    def one_tile(packed):
        column, factor = packed

        def advance(current, operator):
            stepped = jnp.dot(operator.T, current, preferred_element_type=jnp.float32)
            return (stepped * factor).astype(jnp.bfloat16), None

        return lax.scan(advance, column, ops_part)[0]

    result = lax.map(one_tile, (columns, factors))
    return result.transpose(1, 0, 2).reshape(LEV, CELLS)


def reference(adjoint_state, tangent_coef, column_ops, surf_read, surf_write, remap_weights, pair_atmos, pair_ocean, list_len, ocean_owned):
    blocks = BLOCKS_DEV
    slot_count = TILES * CAP
    swept_atmos = sweep_section(adjoint_state[0], tangent_coef[0], column_ops[0])
    swept_ocean = sweep_section(adjoint_state[1], tangent_coef[1], column_ops[1])
    surface_atmos = jnp.dot(surf_read[0], adjoint_state[0], preferred_element_type=jnp.float32).astype(jnp.bfloat16)
    surface_ocean = jnp.dot(surf_read[1], adjoint_state[1], preferred_element_type=jnp.float32).astype(jnp.bfloat16)
    atmos_blocks = surface_atmos.reshape(NF, TILES * blocks, BLK).transpose(1, 0, 2)
    ocean_blocks = surface_ocean.reshape(NF, TILES * blocks, BLK).transpose(1, 0, 2)
    position_of = jnp.zeros((TILES * blocks,), jnp.int32).at[ocean_owned.reshape(-1)].set(
        (jnp.arange(TILES * blocks, dtype=jnp.int32) % blocks).astype(jnp.int32))
    dest_tile = jnp.broadcast_to(jnp.arange(TILES, dtype=jnp.int32)[None, :, None], (TILES, TILES, CAP))
    ocean_seg = (dest_tile * blocks + position_of[pair_ocean]).astype(jnp.int32)
    source_tile = jnp.broadcast_to(jnp.arange(TILES, dtype=jnp.int32)[:, None, None], (TILES, TILES, CAP))
    atmos_seg = (source_tile * blocks + pair_atmos).astype(jnp.int32)
    live_mask = jnp.arange(CAP, dtype=jnp.int32)[None, None, :] < list_len[:, :, None]

    def per_source(packed):
        weights_t, atmos_t, ocean_t, live_t = packed
        weights = weights_t.reshape(slot_count, BLK, BLK).astype(jnp.float32)
        picked = atmos_blocks[atmos_t.reshape(-1)].astype(jnp.float32)
        flux = jnp.einsum("snj,sjm->snm", picked, weights)
        flux = jnp.where(live_t.reshape(slot_count, 1, 1), flux, 0.0)
        echoes = ocean_blocks[ocean_t.reshape(-1)].astype(jnp.float32)
        back = jnp.einsum("sjm,snm->snj", weights, echoes)
        back = jnp.where(live_t.reshape(slot_count, 1, 1), back, 0.0)
        return flux, back

    flux_terms, back_terms = lax.map(per_source, (remap_weights, atmos_seg, ocean_seg, live_mask))
    ocean_sum = jax.ops.segment_sum(flux_terms.reshape(-1, NF * BLK), ocean_seg.reshape(-1), num_segments=TILES * blocks)
    ocean_forcing = ocean_sum.reshape(TILES * blocks, NF, BLK).transpose(1, 0, 2).reshape(NF, CELLS)
    atmos_sum = jax.ops.segment_sum(back_terms.reshape(-1, NF * BLK), atmos_seg.reshape(-1), num_segments=TILES * blocks)
    atmos_forcing = atmos_sum.reshape(TILES * blocks, NF, BLK).transpose(1, 0, 2).reshape(NF, CELLS)
    out_atmos = swept_atmos.astype(jnp.float32) + jnp.dot(surf_write[0], atmos_forcing, precision=lax.Precision.HIGHEST)
    out_ocean = swept_ocean.astype(jnp.float32) + jnp.dot(surf_write[1], ocean_forcing, precision=lax.Precision.HIGHEST)
    return jnp.stack([out_atmos, out_ocean]).astype(jnp.bfloat16)
```

```python
import jax
import jax.numpy as jnp
from jax import lax
from jax.experimental import pallas as pl
from jax.experimental.pallas import tpu as pltpu
from jax.sharding import PartitionSpec as P

NF = 4
BLK = 64
NSTEP = 16
LANES = 128
GROUP = 8
BF16 = jnp.bfloat16
F32 = jnp.float32


def lanes_below(shape, edge):
    return lax.broadcasted_iota(jnp.int32, shape, len(shape) - 1) < edge


def surface_kernel(read_ref, state_ref, out_ref, held):
    step = pl.program_id(0)
    width = state_ref.shape[1]
    tiles = width // LANES
    fields = jnp.dot(read_ref[...], state_ref[...], preferred_element_type=F32)
    for tile in range(tiles):
        row = pl.multiple_of((step * tiles + tile) * 8, 8)
        held[pl.ds(row, NF), :] = fields[:, tile * LANES : (tile + 1) * LANES]

    @pl.when(step == pl.num_programs(0) - 1)
    def _():
        pairs = out_ref.shape[0] // 2
        left = lanes_below((pairs, LANES), BLK)
        for duo in range(NF // 2):
            first = held[pl.ds(2 * duo, pairs, stride=8), :]
            second = held[pl.ds(2 * duo + 1, pairs, stride=8), :]
            cols = slice(duo * LANES, (duo + 1) * LANES)
            even = jnp.where(left, first, pltpu.roll(second, BLK, 1))
            odd = jnp.where(left, pltpu.roll(first, BLK, 1), second)
            out_ref[:pairs, cols] = even.astype(BF16)
            out_ref[pairs:, cols] = odd.astype(BF16)


def surface_blocks(read, state, width=4096):
    levels, cells = state.shape
    blocks = cells // BLK
    return pl.pallas_call(
        surface_kernel,
        grid=(cells // width,),
        out_shape=jax.ShapeDtypeStruct((blocks, NF * BLK), BF16),
        in_specs=[
            pl.BlockSpec((NF, levels), lambda i: (0, 0)),
            pl.BlockSpec((levels, width), lambda i: (0, i)),
        ],
        out_specs=pl.BlockSpec((blocks, NF * BLK), lambda i: (0, 0)),
        scratch_shapes=[pltpu.VMEM((blocks // 2 * 8, LANES), F32)],
        name="surface",
    )(read, state)


def fill_spread(spread):
    row = lax.broadcasted_iota(jnp.int32, spread.shape, 0)
    col = lax.broadcasted_iota(jnp.int32, spread.shape, 1)
    source = (col >> 10) * BLK + ((col >> 4) & 15) * 4 + ((col >> 8) & 3)
    spread[...] = jnp.where(row == source, 1.0, 0.0).astype(BF16)


def own_slot(rows, cols):
    row = lax.broadcasted_iota(jnp.int32, (rows, cols), 0)
    col = lax.broadcasted_iota(jnp.int32, (rows, cols), 1)
    return (row & 15) == (col & 15)


def stacked_weights(weights_ref, tile):
    width = 4 * BLK
    return jnp.concatenate(
        [weights_ref[tile, :, q * width : (q + 1) * width] for q in range(BLK // 4)], 0
    )


def outgoing_kernel(section_ref, key_ref, table_ref, blocks_ref, weights_ref, out_ref, spread):
    step = pl.program_id(0)
    rows = LANES
    blocks = blocks_ref.shape[0]
    key = jnp.broadcast_to(key_ref[pl.ds(step, 1), :], (rows, rows)).T
    pieces = []
    for start in range(0, blocks, LANES):
        stop = min(start + LANES, blocks)
        piece = jnp.where(key == table_ref[:, start : start + LANES], 1.0, 0.0).astype(BF16)
        pieces.append(piece[:, : stop - start])
    chosen = jnp.dot(
        jnp.concatenate(pieces, 1), blocks_ref[...], preferred_element_type=F32
    ).astype(BF16)

    @pl.when(section_ref[0] == 0)
    def _():
        out_ref[...] = chosen

    @pl.when(section_ref[0] == 1)
    def _():
        @pl.when(step == 0)
        def _():
            fill_spread(spread)

        mine = own_slot(rows, spread.shape[1])
        spaced = []
        for duo in range(NF // 2):
            wide = jnp.dot(
                chosen[:, duo * LANES : (duo + 1) * LANES], spread[...], preferred_element_type=F32
            )
            spaced.append(jnp.where(mine, wide, 0.0).astype(BF16))
        left = lanes_below((16, LANES), BLK)
        for tile in range(GROUP):
            slots = slice(tile * 16, (tile + 1) * 16)
            operand = jnp.concatenate(
                [
                    spaced[duo][slots, part * 256 : (part + 1) * 256]
                    for duo in range(NF // 2)
                    for part in range(8)
                ],
                0,
            )
            product = jnp.dot(
                operand, stacked_weights(weights_ref, tile), preferred_element_type=F32
            )
            sums = []
            for field in range(NF):
                quarter = [
                    product[field * 64 + k * 16 : field * 64 + (k + 1) * 16] for k in range(4)
                ]
                total = jnp.where(left, quarter[0][:, :LANES], quarter[1][:, :LANES]) + jnp.where(
                    left, quarter[2][:, LANES:], quarter[3][:, LANES:]
                )
                sums.append(total + pltpu.roll(total, BLK, 1))
            for duo in range(NF // 2):
                out_ref[slots, duo * LANES : (duo + 1) * LANES] = jnp.where(
                    left, sums[2 * duo], sums[2 * duo + 1]
                ).astype(BF16)


def outgoing(section, key, table, blocks, weights):
    lists, cap, square = weights.shape
    slots = lists * cap
    count, width = blocks.shape
    return pl.pallas_call(
        outgoing_kernel,
        out_shape=jax.ShapeDtypeStruct((slots, width), BF16),
        grid_spec=pltpu.PrefetchScalarGridSpec(
            num_scalar_prefetch=1,
            grid=(lists // GROUP,),
            in_specs=[
                pl.BlockSpec(key.shape, lambda i, sec: (0, 0)),
                pl.BlockSpec(table.shape, lambda i, sec: (0, 0)),
                pl.BlockSpec((count, width), lambda i, sec: (0, 0)),
                pl.BlockSpec((GROUP, cap, square), lambda i, sec: (i * sec[0], 0, 0)),
            ],
            out_specs=pl.BlockSpec((GROUP * cap, width), lambda i, sec: (i, 0)),
            scratch_shapes=[pltpu.VMEM((LANES, 2048), BF16)],
        ),
        name="outgoing",
    )(section, key, table, blocks, weights)


def incoming_kernel(
    section_ref, key_ref, table_ref, arrived_ref, weights_ref, out_ref, spread, masked, terms
):
    step = pl.program_id(0)
    rows = LANES
    here = pl.ds(pl.multiple_of(step * rows, rows), rows)

    @pl.when(section_ref[0] == 1)
    def _():
        terms[here, :] = arrived_ref[...]

    @pl.when(section_ref[0] == 0)
    def _():
        @pl.when(step == 0)
        def _():
            fill_spread(spread)

        left = lanes_below((rows, LANES), BLK)
        low, high = [], []
        for duo in range(NF // 2):
            both = arrived_ref[:, duo * LANES : (duo + 1) * LANES].astype(F32)
            turned = pltpu.roll(both, BLK, 1)
            low += [jnp.where(left, both, 0.0).astype(BF16), jnp.where(left, turned, 0.0).astype(BF16)]
            high += [jnp.where(left, 0.0, turned).astype(BF16), jnp.where(left, 0.0, both).astype(BF16)]
        blank = jnp.zeros((16, LANES), BF16)
        mine = own_slot(256, 256)
        for tile in range(GROUP):
            slots = slice(tile * 16, (tile + 1) * 16)
            lines = []
            for field in range(NF):
                lo, hi = low[field][slots], high[field][slots]
                lines += [
                    jnp.concatenate([lo, blank], 1),
                    jnp.concatenate([hi, blank], 1),
                    jnp.concatenate([blank, lo], 1),
                    jnp.concatenate([blank, hi], 1),
                ]
            product = lax.dot_general(
                jnp.concatenate(lines, 0),
                stacked_weights(weights_ref, tile),
                (((1,), (1,)), ((), ())),
                preferred_element_type=F32,
            )
            kept = jnp.where(mine, product, 0.0).astype(BF16)
            for part in range(4 * NF):
                masked[slots, part * 256 : (part + 1) * 256] = kept[part * 16 : (part + 1) * 16]
        for duo in range(NF // 2):
            terms[here, duo * LANES : (duo + 1) * LANES] = lax.dot_general(
                masked[:, duo * 2048 : (duo + 1) * 2048],
                spread[...],
                (((1,), (1,)), ((), ())),
                preferred_element_type=F32,
            ).astype(BF16)

    @pl.when(step == pl.num_programs(0) - 1)
    def _():
        slots = terms.shape[0]
        count = out_ref.shape[0] // 4
        table = jnp.broadcast_to(table_ref[...], (LANES, table_ref.shape[1])).T[:count]
        picks = [
            jnp.where(table == key_ref[r : r + 1, :], 1.0, 0.0).astype(BF16)
            for r in range(slots // LANES)
        ]
        total = jnp.dot(jnp.concatenate(picks, 1), terms[...], preferred_element_type=F32)
        pairs = count // 2
        left = lanes_below((pairs, LANES), BLK)
        for duo in range(NF // 2):
            even = total[:pairs, duo * LANES : (duo + 1) * LANES]
            odd = total[pairs:, duo * LANES : (duo + 1) * LANES]
            fields = (
                jnp.where(left, even, pltpu.roll(odd, BLK, 1)),
                jnp.where(left, pltpu.roll(even, BLK, 1), odd),
            )
            for n, field in enumerate(fields):
                coarse = field.astype(BF16).astype(F32)
                out_ref[pl.ds(2 * duo + n, pairs, stride=8), :] = coarse
                out_ref[pl.ds(NF + 2 * duo + n, pairs, stride=8), :] = field - coarse


def incoming(section, key, table, arrived, weights, blocks):
    lists, cap, square = weights.shape
    slots, width = arrived.shape
    return pl.pallas_call(
        incoming_kernel,
        out_shape=jax.ShapeDtypeStruct((blocks // 2 * 8, LANES), F32),
        grid_spec=pltpu.PrefetchScalarGridSpec(
            num_scalar_prefetch=1,
            grid=(lists // GROUP,),
            in_specs=[
                pl.BlockSpec(key.shape, lambda i, sec: (0, 0)),
                pl.BlockSpec(table.shape, lambda i, sec: (0, 0)),
                pl.BlockSpec((GROUP * cap, width), lambda i, sec: (i, 0)),
                pl.BlockSpec((GROUP, cap, square), lambda i, sec: (i * (1 - sec[0]), 0, 0)),
            ],
            out_specs=pl.BlockSpec((blocks // 2 * 8, LANES), lambda i, sec: (0, 0)),
            scratch_shapes=[
                pltpu.VMEM((LANES, 2048), BF16),
                pltpu.VMEM((GROUP * cap, 4096), BF16),
                pltpu.VMEM((slots, width), BF16),
            ],
        ),
        name="incoming",
    )(section, key, table, arrived, weights)


def sweep_kernel(ops_ref, state_ref, coef_ref, out_ref):
    current = state_ref[...]
    factors = coef_ref[...].astype(F32)
    for step in range(NSTEP):
        stepped = jnp.dot(ops_ref[step], current, preferred_element_type=F32)
        current = (stepped * factors).astype(BF16)
    out_ref[...] = current


def sweep(ops, state, coef, width=4096):
    levels, cells = state.shape
    return pl.pallas_call(
        sweep_kernel,
        grid=(cells // width,),
        out_shape=jax.ShapeDtypeStruct((levels, cells), BF16),
        in_specs=[
            pl.BlockSpec(ops.shape, lambda i: (0, 0, 0)),
            pl.BlockSpec((levels, width), lambda i: (0, i)),
            pl.BlockSpec((levels, width), lambda i: (0, i)),
        ],
        out_specs=pl.BlockSpec((levels, width), lambda i: (0, i)),
        compiler_params=pltpu.CompilerParams(vmem_limit_bytes=48 << 20),
        name="sweep",
    )(ops, state, coef)


def finish_kernel(write_ref, forcing_ref, swept_ref, out_ref):
    tiles = swept_ref.shape[1] // LANES
    forcing = jnp.concatenate([forcing_ref[t * 8 : (t + 1) * 8, :] for t in range(tiles)], 1)
    operand = jnp.concatenate([forcing, forcing], 0).astype(BF16)
    added = jnp.dot(write_ref[...], operand, preferred_element_type=F32)
    out_ref[...] = (swept_ref[...].astype(F32) + added).astype(BF16)


def finish(write, forcing, swept, width=4096):
    levels, cells = swept.shape
    return pl.pallas_call(
        finish_kernel,
        grid=(cells // width,),
        out_shape=jax.ShapeDtypeStruct((levels, cells), BF16),
        in_specs=[
            pl.BlockSpec(write.shape, lambda i: (0, 0)),
            pl.BlockSpec((width // LANES * 8, LANES), lambda i: (i, 0)),
            pl.BlockSpec((levels, width), lambda i: (0, i)),
        ],
        out_specs=pl.BlockSpec((levels, width), lambda i: (0, i)),
        name="finish",
    )(write, forcing, swept)


def body(
    adjoint_state,
    tangent_coef,
    column_ops,
    surf_read,
    surf_write,
    remap_weights,
    pair_atmos,
    pair_ocean,
    list_len,
    ocean_owned,
):
    section = lax.axis_index("sec")
    lists, cap = pair_atmos.shape[1:]
    blocks = ocean_owned.shape[1]
    pairs = blocks // 2
    state = adjoint_state[0]
    arrived_ids = lax.all_to_all(pair_ocean[0], "tile", split_axis=0, concat_axis=0, tiled=True)

    surface = surface_blocks(surf_read[0], state)
    partner = lax.ppermute(surface, "sec", [(0, 1), (1, 0)])

    live = lax.broadcasted_iota(jnp.int32, (lists, cap), 1) < list_len[0][:, None]
    atmos = pair_atmos[0]
    atmos_key = jnp.where(live, (atmos & 1) * pairs + (atmos >> 1), -1)
    keys = (lists * cap // LANES, LANES)
    atmos_key = atmos_key.reshape(keys).astype(F32)
    ocean_key = arrived_ids.reshape(keys).astype(F32)
    padded = -(-blocks // LANES) * LANES
    owned = jnp.pad(ocean_owned[0].reshape(pairs, 2).T.reshape(1, blocks), ((0, 0), (0, padded - blocks)), constant_values=-2)
    owned_table = owned.astype(F32)
    plain_table = lax.broadcasted_iota(jnp.int32, (1, padded), 1).astype(F32)
    first = section == 0
    out_key = jnp.where(first, ocean_key, atmos_key)
    in_key = jnp.where(first, atmos_key, ocean_key)
    out_table = jnp.where(first, owned_table, plain_table)
    in_table = jnp.where(first, plain_table, owned_table)
    which = section.reshape(1).astype(jnp.int32)

    payload = outgoing(which, out_key, out_table, partner, remap_weights[0])
    received = lax.all_to_all(
        payload.reshape(lists, cap, NF * BLK), "tile", split_axis=0, concat_axis=0, tiled=True
    )
    swept = sweep(column_ops[0].transpose(0, 2, 1), state, tangent_coef[0])
    forcing = incoming(
        which, in_key, in_table, received.reshape(lists * cap, NF * BLK), remap_weights[0], blocks
    )
    write = surf_write[0]
    coarse = lax.reduce_precision(write, 8, 7)
    fine = write - coarse
    operand = jnp.concatenate([coarse, coarse, fine, fine], 1).astype(BF16)
    return finish(operand, forcing, swept)[None]


def solution(mesh):
    in_specs = (
        P("sec", None, "tile"),
        P("sec", None, "tile"),
        P("sec", None, None, None),
        P("sec", None, None),
        P("sec", None, None),
        P("tile", None, None, None),
        P("tile", None, None),
        P("tile", None, None),
        P("tile", None),
        P("tile", None),
    )
    out_specs = P("sec", None, "tile")
    return jax.shard_map(body, mesh=mesh, in_specs=in_specs, out_specs=out_specs, check_vma=False)
```

```python
import jax
import jax.numpy as jnp
from jax import lax
from jax.experimental import pallas as pl
from jax.experimental.pallas import tpu as pltpu
from jax.sharding import PartitionSpec as P

NF = 4
BLK = 64
NSTEP = 16
LANES = 128
GROUP = 8
SPLIT = 2048
STRIDE = 3 * SPLIT
VMEM_LIMIT = 56 << 20
BF16 = jnp.bfloat16
F32 = jnp.float32


def lanes_below(shape, edge):
    return lax.broadcasted_iota(jnp.int32, shape, len(shape) - 1) < edge


def surface_kernel(read_ref, state_hbm, out_ref, state, held, sems):
    parts = sems.shape[0]
    width = state.shape[1] // parts
    tiles = width // LANES

    def fetch(part):
        cols = pl.ds(pl.multiple_of(part * width, width), width)
        return pltpu.make_async_copy(state_hbm.at[:, cols], state.at[:, cols], sems.at[part])

    for part in range(parts):
        fetch(part).start()

    def compute(part, carry):
        fetch(part).wait()
        cols = pl.ds(pl.multiple_of(part * width, width), width)
        fields = jnp.dot(read_ref[...], state[:, cols], preferred_element_type=F32)
        for tile in range(tiles):
            row = pl.multiple_of((part * tiles + tile) * 8, 8)
            held[pl.ds(row, NF), :] = fields[:, tile * LANES : (tile + 1) * LANES]
        return carry

    lax.fori_loop(0, parts, compute, 0)
    pairs = out_ref.shape[0] // 2
    left = lanes_below((pairs, LANES), BLK)
    for duo in range(NF // 2):
        first = held[pl.ds(2 * duo, pairs, stride=8), :]
        second = held[pl.ds(2 * duo + 1, pairs, stride=8), :]
        cols = slice(duo * LANES, (duo + 1) * LANES)
        even = jnp.where(left, first, pltpu.roll(second, BLK, 1))
        odd = jnp.where(left, pltpu.roll(first, BLK, 1), second)
        out_ref[:pairs, cols] = even.astype(BF16)
        out_ref[pairs:, cols] = odd.astype(BF16)


def surface_blocks(read, state, parts=9):
    levels, cells = state.shape
    blocks = cells // BLK
    return pl.pallas_call(
        surface_kernel,
        out_shape=jax.ShapeDtypeStruct((blocks, NF * BLK), BF16),
        in_specs=[
            pl.BlockSpec(memory_space=pltpu.VMEM),
            pl.BlockSpec(memory_space=pl.ANY),
        ],
        out_specs=pl.BlockSpec(memory_space=pltpu.VMEM),
        scratch_shapes=[
            pltpu.VMEM((levels, cells), BF16),
            pltpu.VMEM((blocks // 2 * 8, LANES), F32),
            pltpu.SemaphoreType.DMA((parts,)),
        ],
        compiler_params=pltpu.CompilerParams(vmem_limit_bytes=VMEM_LIMIT),
        name="surface",
    )(read, state)


def fetch_weights(weights_hbm, weights, sems, part):
    lists = pl.ds(part * GROUP, GROUP)
    return pltpu.make_async_copy(weights_hbm.at[lists], weights.at[lists], sems.at[part])


def half_list(weights, tile, half):
    return jnp.concatenate(
        [weights[tile, half, :, q * LANES : (q + 1) * LANES] for q in range(BLK // 2)], 0
    )


def pick(values, lanes):
    return jnp.take_along_axis(values, lanes, axis=1, mode="promise_in_bounds")


def outgoing_kernel(
    section_ref, key_ref, table_ref, blocks_ref, weights_hbm, out_ref, weights, chosen, sems
):
    parts = sems.shape[0]
    blocks = blocks_ref.shape[0]
    forward = section_ref[0] == 1

    @pl.when(forward)
    def _():
        for part in range(parts):
            fetch_weights(weights_hbm, weights, sems, part).start()

    for part in range(parts):
        key = jnp.broadcast_to(key_ref[part : part + 1, :], (LANES, LANES)).T
        pieces = []
        for start in range(0, blocks, LANES):
            stop = min(start + LANES, blocks)
            piece = jnp.where(key == table_ref[:, start : start + LANES], 1.0, 0.0).astype(BF16)
            pieces.append(piece[:, : stop - start])
        chosen[part * LANES : (part + 1) * LANES, :] = jnp.dot(
            jnp.concatenate(pieces, 1), blocks_ref[...], preferred_element_type=F32
        )

    @pl.when(jnp.logical_not(forward))
    def _():
        out_ref[...] = chosen[...].astype(BF16)

    @pl.when(forward)
    def _():
        lane = lax.broadcasted_iota(jnp.int32, (8, LANES), 1)
        row = lax.broadcasted_iota(jnp.int32, (8, LANES), 0)
        own = (lane & 7) == row
        left = lane < BLK

        def lists(part, carry):
            fetch_weights(weights_hbm, weights, sems, part).wait()
            for inner in range(GROUP):
                tile = part * GROUP + inner
                rows = pl.ds(pl.multiple_of(tile * 16, 16), 16)
                values = chosen[rows, :]
                results = []
                for half in range(2):
                    lines = []
                    for field in range(NF):
                        duo = values[
                            half * 8 : half * 8 + 8, field // 2 * LANES : (field // 2 + 1) * LANES
                        ]
                        for parity in range(2):
                            line = []
                            for side in range(2):
                                source = (field % 2) * BLK + 2 * (side * 16 + (lane >> 3)) + parity
                                line.append(jnp.where(own, pick(duo, source), 0.0))
                            lines.append(jnp.concatenate(line, 1))
                    product = jnp.dot(
                        jnp.concatenate(lines, 0).astype(BF16),
                        half_list(weights, tile, half),
                        preferred_element_type=F32,
                    )
                    sums = []
                    for field in range(NF):
                        even = product[field * 16 : field * 16 + 8]
                        odd = product[field * 16 + 8 : field * 16 + 16]
                        total = jnp.where(left, even, odd)
                        sums.append(total + pltpu.roll(total, BLK, 1))
                    results.append(
                        [jnp.where(left, sums[2 * duo], sums[2 * duo + 1]) for duo in range(NF // 2)]
                    )
                for duo in range(NF // 2):
                    out_ref[rows, duo * LANES : (duo + 1) * LANES] = jnp.concatenate(
                        [results[0][duo], results[1][duo]], 0
                    ).astype(BF16)
            return carry

        lax.fori_loop(0, parts, lists, 0)


def outgoing(section, key, table, blocks, weights):
    lists, halves, cap, square = weights.shape
    slots = lists * halves * cap
    width = blocks.shape[1]
    return pl.pallas_call(
        outgoing_kernel,
        out_shape=jax.ShapeDtypeStruct((slots, width), BF16),
        in_specs=[
            pl.BlockSpec(memory_space=pltpu.SMEM),
            pl.BlockSpec(memory_space=pltpu.VMEM),
            pl.BlockSpec(memory_space=pltpu.VMEM),
            pl.BlockSpec(memory_space=pltpu.VMEM),
            pl.BlockSpec(memory_space=pl.ANY),
        ],
        out_specs=pl.BlockSpec(memory_space=pltpu.VMEM),
        scratch_shapes=[
            pltpu.VMEM(weights.shape, BF16),
            pltpu.VMEM((slots, width), F32),
            pltpu.SemaphoreType.DMA((lists // GROUP,)),
        ],
        compiler_params=pltpu.CompilerParams(vmem_limit_bytes=VMEM_LIMIT),
        name="outgoing",
    )(section, key, table, blocks, weights)


def advance(ops_ref, states, coefs):
    current = jnp.concatenate([ref[...] for ref in states], 1)
    factors = jnp.concatenate([ref[...].astype(F32) for ref in coefs], 1)
    for step in range(NSTEP):
        stepped = jnp.dot(ops_ref[step], current, preferred_element_type=F32)
        current = (stepped * factors).astype(BF16)
    return current


def early_kernel(ops_ref, state_a, state_b, coef_a, coef_b, out_ref):
    out_ref[...] = advance(ops_ref, (state_a, state_b), (coef_a, coef_b))


def early_sweep(ops, state, coef):
    levels, cells = state.shape
    steps = cells // STRIDE // 2
    ratio = STRIDE // SPLIT
    first = pl.BlockSpec((levels, SPLIT), lambda i: (0, 2 * i * ratio))
    second = pl.BlockSpec((levels, SPLIT), lambda i: (0, (2 * i + 1) * ratio))
    return pl.pallas_call(
        early_kernel,
        grid=(steps,),
        out_shape=jax.ShapeDtypeStruct((levels, cells // ratio), BF16),
        in_specs=[pl.BlockSpec(ops.shape, lambda i: (0, 0, 0)), first, second, first, second],
        out_specs=pl.BlockSpec((levels, 2 * SPLIT), lambda i: (0, i)),
        compiler_params=pltpu.CompilerParams(vmem_limit_bytes=VMEM_LIMIT),
        name="early",
    )(ops, state, state, coef, coef)


def backward_lists(arrived_ref, weights_hbm, weights, terms, sems):
    lane = lax.broadcasted_iota(jnp.int32, (8, LANES), 1)
    row = lax.broadcasted_iota(jnp.int32, (8, LANES), 0)
    left = lane < BLK
    source = (((lane >> 1) & 15) << 3) + row
    half_kind = ((lane >> 5) & 1) * 2 + (lane & 1)

    def lists(part, carry):
        fetch_weights(weights_hbm, weights, sems, part).wait()
        for inner in range(GROUP):
            tile = part * GROUP + inner
            rows = pl.ds(pl.multiple_of(tile * 16, 16), 16)
            echoes = arrived_ref[rows, :].astype(F32)
            results = []
            for half in range(2):
                lines = []
                for duo in range(NF // 2):
                    both = echoes[half * 8 : half * 8 + 8, duo * LANES : (duo + 1) * LANES]
                    turned = pltpu.roll(both, BLK, 1)
                    lines += [
                        jnp.where(left, both, 0.0),
                        jnp.where(left, 0.0, turned),
                        jnp.where(left, turned, 0.0),
                        jnp.where(left, 0.0, both),
                    ]
                product = lax.dot_general(
                    jnp.concatenate(lines, 0).astype(BF16),
                    half_list(weights, tile, half),
                    (((1,), (1,)), ((), ())),
                    preferred_element_type=F32,
                )
                outs = []
                for duo in range(NF // 2):
                    fields = []
                    for field in (2 * duo, 2 * duo + 1):
                        total = None
                        for side in range(2):
                            for parity in range(2):
                                start = field * 16 + parity * 8
                                value = pick(
                                    product[start : start + 8, side * LANES : (side + 1) * LANES],
                                    source,
                                )
                                kind = side * 2 + parity
                                total = (
                                    value
                                    if total is None
                                    else jnp.where(half_kind == kind, value, total)
                                )
                        fields.append(total)
                    outs.append(jnp.where(left, fields[0], fields[1]))
                results.append(outs)
            for duo in range(NF // 2):
                terms[rows, duo * LANES : (duo + 1) * LANES] = jnp.concatenate(
                    [results[0][duo], results[1][duo]], 0
                ).astype(BF16)
        return carry

    lax.fori_loop(0, sems.shape[0], lists, 0)


def sum_terms(key_ref, table_ref, terms, forcing):
    slots = terms.shape[0]
    pairs = forcing.shape[0] // 8
    table = jnp.broadcast_to(table_ref[...], (LANES, table_ref.shape[1])).T[: 2 * pairs]
    picks = [
        jnp.where(table == key_ref[r : r + 1, :], 1.0, 0.0).astype(BF16)
        for r in range(slots // LANES)
    ]
    total = jnp.dot(jnp.concatenate(picks, 1), terms[...], preferred_element_type=F32)
    left = lanes_below((pairs, LANES), BLK)
    for duo in range(NF // 2):
        even = total[:pairs, duo * LANES : (duo + 1) * LANES]
        odd = total[pairs:, duo * LANES : (duo + 1) * LANES]
        fields = (
            jnp.where(left, even, pltpu.roll(odd, BLK, 1)),
            jnp.where(left, pltpu.roll(even, BLK, 1), odd),
        )
        for n, field in enumerate(fields):
            coarse = field.astype(BF16).astype(F32)
            forcing[pl.ds(2 * duo + n, pairs, stride=8), :] = coarse
            forcing[pl.ds(NF + 2 * duo + n, pairs, stride=8), :] = field - coarse


def late_kernel(
    section_ref,
    key_ref,
    table_ref,
    arrived_ref,
    weights_hbm,
    write_ref,
    ops_ref,
    swept_ref,
    state_a,
    state_b,
    coef_a,
    coef_b,
    out_ref,
    weights,
    terms,
    forcing,
    sems,
):
    step = pl.program_id(0)
    parts = sems.shape[0]

    @pl.when(step == 0)
    def _():
        @pl.when(section_ref[0] == 0)
        def _():
            for part in range(parts):
                fetch_weights(weights_hbm, weights, sems, part).start()
            backward_lists(arrived_ref, weights_hbm, weights, terms, sems)

        @pl.when(section_ref[0] == 1)
        def _():
            terms[...] = arrived_ref[...]

        sum_terms(key_ref, table_ref, terms, forcing)

    tiles = STRIDE // LANES
    base = step * tiles
    pieces = [
        forcing[pl.ds(pl.multiple_of((base + t) * 8, 8), 8), :] for t in range(tiles)
    ]
    fields = jnp.concatenate(pieces, 1)
    operand = jnp.concatenate([fields, fields], 0).astype(BF16)
    added = jnp.dot(write_ref[...], operand, preferred_element_type=F32)
    out_ref[:, :SPLIT] = (swept_ref[...].astype(F32) + added[:, :SPLIT]).astype(BF16)
    current = advance(ops_ref, (state_a, state_b), (coef_a, coef_b))
    out_ref[:, SPLIT:] = (current.astype(F32) + added[:, SPLIT:]).astype(BF16)


def late(section, key, table, arrived, weights, write, ops, swept, state, coef):
    levels, cells = state.shape
    lists, halves, cap, square = weights.shape
    slots, width = arrived.shape
    ratio = STRIDE // SPLIT
    whole = pl.BlockSpec(memory_space=pltpu.VMEM)
    second = pl.BlockSpec((levels, SPLIT), lambda i: (0, i * ratio + 1))
    third = pl.BlockSpec((levels, SPLIT), lambda i: (0, i * ratio + 2))
    return pl.pallas_call(
        late_kernel,
        grid=(cells // STRIDE,),
        out_shape=jax.ShapeDtypeStruct((levels, cells), BF16),
        in_specs=[
            pl.BlockSpec(memory_space=pltpu.SMEM),
            whole,
            whole,
            whole,
            pl.BlockSpec(memory_space=pl.ANY),
            whole,
            whole,
            pl.BlockSpec((levels, SPLIT), lambda i: (0, i)),
            second,
            third,
            second,
            third,
        ],
        out_specs=pl.BlockSpec((levels, STRIDE), lambda i: (0, i)),
        scratch_shapes=[
            pltpu.VMEM(weights.shape, BF16),
            pltpu.VMEM((slots, width), BF16),
            pltpu.VMEM((cells // LANES * 8, LANES), F32),
            pltpu.SemaphoreType.DMA((lists // GROUP,)),
        ],
        compiler_params=pltpu.CompilerParams(vmem_limit_bytes=VMEM_LIMIT),
        name="late",
    )(section, key, table, arrived, weights, write, ops, swept, state, state, coef, coef)


def body(
    adjoint_state,
    tangent_coef,
    column_ops,
    surf_read,
    surf_write,
    remap_weights,
    pair_atmos,
    pair_ocean,
    list_len,
    ocean_owned,
):
    section = lax.axis_index("sec")
    lists, cap = pair_atmos.shape[1:]
    blocks = ocean_owned.shape[1]
    pairs = blocks // 2
    state = adjoint_state[0]
    arrived_ids = lax.all_to_all(pair_ocean[0], "tile", split_axis=0, concat_axis=0, tiled=True)

    surface = surface_blocks(surf_read[0], state)
    partner = lax.ppermute(surface, "sec", [(0, 1), (1, 0)])

    live = lax.broadcasted_iota(jnp.int32, (lists, cap), 1) < list_len[0][:, None]
    atmos = pair_atmos[0]
    atmos_key = jnp.where(live, (atmos & 1) * pairs + (atmos >> 1), -1)
    keys = (lists * cap // LANES, LANES)
    atmos_key = atmos_key.reshape(keys).astype(F32)
    ocean_key = arrived_ids.reshape(keys).astype(F32)
    padded = -(-blocks // LANES) * LANES
    owned = jnp.pad(ocean_owned[0].reshape(pairs, 2).T.reshape(1, blocks), ((0, 0), (0, padded - blocks)), constant_values=-2)
    owned_table = owned.astype(F32)
    plain_table = lax.broadcasted_iota(jnp.int32, (1, padded), 1).astype(F32)
    first = section == 0
    out_key = jnp.where(first, ocean_key, atmos_key)
    in_key = jnp.where(first, atmos_key, ocean_key)
    out_table = jnp.where(first, owned_table, plain_table)
    in_table = jnp.where(first, plain_table, owned_table)
    which = section.reshape(1).astype(jnp.int32)

    weights = remap_weights[0].reshape(lists, cap // 8, 8, BLK * BLK)
    payload = outgoing(which, out_key, out_table, partner, weights)
    received = lax.all_to_all(
        payload.reshape(lists, cap, NF * BLK), "tile", split_axis=0, concat_axis=0, tiled=True
    )
    ops = column_ops[0].transpose(0, 2, 1)
    swept = early_sweep(ops, state, tangent_coef[0])
    write = surf_write[0]
    coarse = lax.reduce_precision(write, 8, 7)
    fine = write - coarse
    operand = jnp.concatenate([coarse, coarse, fine, fine], 1).astype(BF16)
    arrived = received.reshape(lists * cap, NF * BLK)
    out = late(
        which, in_key, in_table, arrived, weights, operand, ops, swept, state, tangent_coef[0]
    )
    return out[None]


def solution(mesh):
    in_specs = (
        P("sec", None, "tile"),
        P("sec", None, "tile"),
        P("sec", None, None, None),
        P("sec", None, None),
        P("sec", None, None),
        P("tile", None, None, None),
        P("tile", None, None),
        P("tile", None, None),
        P("tile", None),
        P("tile", None),
    )
    out_specs = P("sec", None, "tile")
    return jax.shard_map(body, mesh=mesh, in_specs=in_specs, out_specs=out_specs, check_vma=False)
```

```python
import jax
import jax.numpy as jnp
from jax import lax
from jax.experimental import pallas as pl
from jax.experimental.pallas import tpu as pltpu
from jax.sharding import PartitionSpec as P

NF = 4
BLK = 64
NSTEP = 16
LANES = 128
GROUP = 8
WIDTH = 4096
FIRST = 2
SECOND = 4
BF16 = jnp.bfloat16
F32 = jnp.float32


def lanes_below(shape, edge):
    return lax.broadcasted_iota(jnp.int32, shape, len(shape) - 1) < edge


def advance(ops_ref, current, coef):
    factors = coef.astype(F32)
    for step in range(NSTEP):
        stepped = jnp.dot(ops_ref[step], current, preferred_element_type=F32)
        current = (stepped * factors).astype(BF16)
    return current


def early_column(block):
    return block // 2 * 3 + block % 2


def surface_kernel(
    read_ref, ops_ref, state_hbm, coef_hbm, out_ref, swept_hbm, state, coef, swept, held, sems
):
    parts = sems.shape[0] - 2
    tiles = WIDTH // LANES

    def columns(part):
        return pl.ds(pl.multiple_of(part * WIDTH, WIDTH), WIDTH)

    def fetch(part):
        return pltpu.make_async_copy(
            state_hbm.at[:, columns(part)], state.at[:, columns(part)], sems.at[part]
        )

    factors = pltpu.make_async_copy(coef_hbm.at[:, pl.ds(0, WIDTH)], coef, sems.at[parts])
    store = pltpu.make_async_copy(swept, swept_hbm.at[:, pl.ds(0, WIDTH)], sems.at[parts + 1])
    fetch(0).start()
    factors.start()
    for part in range(1, parts):
        fetch(part).start()

    def compute(part):
        fields = jnp.dot(read_ref[...], state[:, columns(part)], preferred_element_type=F32)
        for tile in range(tiles):
            row = pl.multiple_of((part * tiles + tile) * 8, 8)
            held[pl.ds(row, NF), :] = fields[:, tile * LANES : (tile + 1) * LANES]

    fetch(0).wait()
    factors.wait()
    swept[...] = advance(ops_ref, state[:, :WIDTH], coef[...])
    store.start()
    compute(0)

    def following(part, carry):
        fetch(part).wait()
        compute(part)
        return carry

    lax.fori_loop(1, parts, following, 0)
    pairs = out_ref.shape[0] // 2
    left = lanes_below((pairs, LANES), BLK)
    for duo in range(NF // 2):
        first = held[pl.ds(2 * duo, pairs, stride=8), :]
        second = held[pl.ds(2 * duo + 1, pairs, stride=8), :]
        cols = slice(duo * LANES, (duo + 1) * LANES)
        even = jnp.where(left, first, pltpu.roll(second, BLK, 1))
        odd = jnp.where(left, pltpu.roll(first, BLK, 1), second)
        out_ref[:pairs, cols] = even.astype(BF16)
        out_ref[pairs:, cols] = odd.astype(BF16)
    store.wait()


def surface_blocks(read, ops, state, coef):
    levels, cells = state.shape
    blocks = cells // BLK
    parts = cells // WIDTH
    whole = pl.BlockSpec(memory_space=pltpu.VMEM)
    there = pl.BlockSpec(memory_space=pl.ANY)
    return pl.pallas_call(
        surface_kernel,
        out_shape=(
            jax.ShapeDtypeStruct((blocks, NF * BLK), BF16),
            pltpu.HBM((levels, cells // 3 * 2), BF16),
        ),
        in_specs=[whole, whole, there, there],
        out_specs=(whole, there),
        scratch_shapes=[
            pltpu.VMEM((levels, cells), BF16),
            pltpu.VMEM((levels, WIDTH), BF16),
            pltpu.VMEM((levels, WIDTH), BF16),
            pltpu.VMEM((blocks // 2 * 8, LANES), F32),
            pltpu.SemaphoreType.DMA((parts + 2,)),
        ],
        compiler_params=pltpu.CompilerParams(vmem_limit_bytes=24 << 20),
        name="surface",
    )(read, ops, state, coef)


def fetch_weights(weights_hbm, weights, sems, part):
    lists = pl.ds(part * GROUP, GROUP)
    return pltpu.make_async_copy(weights_hbm.at[lists], weights.at[lists], sems.at[part])


def half_list(weights, tile, half):
    return jnp.concatenate(
        [weights[tile, half, :, q * LANES : (q + 1) * LANES] for q in range(BLK // 2)], 0
    )


def pick(values, lanes):
    return jnp.take_along_axis(values, lanes, axis=1, mode="promise_in_bounds")


def widened(values):
    rows, cols = values.shape
    return jnp.concatenate([values, jnp.zeros((rows, LANES - cols), values.dtype)], 1)


def slot_rows(values):
    lists = values.shape[0]
    lane = lax.broadcasted_iota(jnp.int32, (lists, LANES), 1)
    row = lax.broadcasted_iota(jnp.int32, (lists, LANES), 0)
    spread = jnp.where((lane >> 4) == (row & 7), pick(widened(values), lane & 15), 0.0)
    return jnp.sum(spread.reshape(lists // 8, 8, LANES), 1)


def even_first(values, padded):
    count = values.shape[1]
    pairs = count // 2
    lane = lax.broadcasted_iota(jnp.int32, (8, LANES), 1)
    sources = []
    for start in range(0, count, LANES):
        source = values[:, start : min(start + LANES, count)]
        sources.append(source if source.shape[1] == LANES else widened(source))
    sources = [jnp.broadcast_to(source, (8, LANES)) for source in sources]
    tiles = []
    for tile in range(padded // LANES):
        spots = [
            2 * j if j < pairs else 2 * (j - pairs) + 1
            for j in range(tile * LANES, min((tile + 1) * LANES, count))
        ]
        at = tile * LANES + lane
        wanted = jnp.where(at < pairs, 2 * at, 2 * (at - pairs) + 1)
        result = jnp.full((8, LANES), -2.0, F32)
        for index in sorted({spot // LANES for spot in spots}):
            inside = ((wanted >> 7) == index) & (at < count)
            result = jnp.where(inside, pick(sources[index], wanted & 127), result)
        tiles.append(result)
    return jnp.concatenate(tiles, 1)[:1]


def outgoing_kernel(
    section_ref,
    atmos_ref,
    length_ref,
    ids_ref,
    owned_ref,
    blocks_ref,
    ops_ref,
    weights_hbm,
    state_hbm,
    coef_hbm,
    swept_in,
    out_ref,
    in_key_ref,
    in_table_ref,
    swept_hbm,
    chosen,
    weights,
    state,
    coef,
    swept,
    weight_sems,
    sems,
):
    count = state.shape[0]

    def fetch(block):
        columns = pl.ds(pl.multiple_of(early_column(FIRST + block) * WIDTH, WIDTH), WIDTH)
        return (
            pltpu.make_async_copy(state_hbm.at[:, columns], state.at[block], sems.at[0, block]),
            pltpu.make_async_copy(coef_hbm.at[:, columns], coef.at[block], sems.at[1, block]),
        )

    def store(block):
        columns = pl.ds(pl.multiple_of((FIRST + block) * WIDTH, WIDTH), WIDTH)
        return pltpu.make_async_copy(
            swept.at[block], swept_hbm.at[:, columns], sems.at[2, block]
        )

    for block in range(count):
        for copy in fetch(block):
            copy.start()

    @pl.when(section_ref[0] == 1)
    def _():
        for part in range(weight_sems.shape[0]):
            fetch_weights(weights_hbm, weights, weight_sems, part).start()

    def sweep_block(block, carry):
        for copy in fetch(block):
            copy.wait()
        swept[block] = advance(ops_ref, state[block], coef[block])
        store(block).start()
        return carry

    lax.fori_loop(0, count, sweep_block, 0)
    blocks = blocks_ref.shape[0]
    pairs = blocks // 2
    padded = in_table_ref.shape[1]
    parts = in_key_ref.shape[0]
    first = section_ref[0] == 0
    lane = lax.broadcasted_iota(jnp.int32, (8, LANES), 1)
    row = lax.broadcasted_iota(jnp.int32, (8, LANES), 0)
    lengths = jnp.broadcast_to(widened(length_ref[...].astype(F32)), (8, LANES))
    live = (lane & 15).astype(F32) < pick(lengths, row * 8 + (lane >> 4))
    atmos = atmos_ref[...]
    atmos = ((atmos & 1) * pairs + (atmos >> 1)).astype(F32)
    atmos_key = jnp.where(live, slot_rows(widened(atmos).T[: atmos.shape[1]]), -1.0)
    ocean_key = slot_rows(ids_ref[:, 0, :].astype(F32))
    owned_table = even_first(owned_ref[...].astype(F32), padded)
    plain_table = lax.broadcasted_iota(jnp.int32, (1, padded), 1).astype(F32)
    out_key = jnp.where(first, ocean_key, atmos_key)
    out_table = jnp.where(first, owned_table, plain_table)
    in_key_ref[...] = jnp.where(first, atmos_key, ocean_key)
    in_table_ref[...] = jnp.where(first, plain_table, owned_table)

    for part in range(parts):
        key = jnp.broadcast_to(out_key[part : part + 1, :], (LANES, LANES)).T
        pieces = []
        for start in range(0, blocks, LANES):
            stop = min(start + LANES, blocks)
            piece = jnp.where(key == out_table[:, start : start + LANES], 1.0, 0.0).astype(BF16)
            pieces.append(piece[:, : stop - start])
        chosen[part * LANES : (part + 1) * LANES, :] = jnp.dot(
            jnp.concatenate(pieces, 1), blocks_ref[...], preferred_element_type=F32
        )

    @pl.when(first)
    def _():
        out_ref[...] = chosen[...].astype(BF16)

    @pl.when(jnp.logical_not(first))
    def _():
        own = (lane & 7) == row
        left = lane < BLK

        def lists(part, carry):
            fetch_weights(weights_hbm, weights, weight_sems, part).wait()
            for inner in range(GROUP):
                tile = part * GROUP + inner
                rows = pl.ds(pl.multiple_of(tile * 16, 16), 16)
                values = chosen[rows, :]
                results = []
                for half in range(2):
                    lines = []
                    for field in range(NF):
                        duo = values[
                            half * 8 : half * 8 + 8, field // 2 * LANES : (field // 2 + 1) * LANES
                        ]
                        for parity in range(2):
                            line = []
                            for side in range(2):
                                source = (field % 2) * BLK + 2 * (side * 16 + (lane >> 3)) + parity
                                line.append(jnp.where(own, pick(duo, source), 0.0))
                            lines.append(jnp.concatenate(line, 1))
                    product = jnp.dot(
                        jnp.concatenate(lines, 0).astype(BF16),
                        half_list(weights, tile, half),
                        preferred_element_type=F32,
                    )
                    sums = []
                    for field in range(NF):
                        even = product[field * 16 : field * 16 + 8]
                        odd = product[field * 16 + 8 : field * 16 + 16]
                        total = jnp.where(left, even, odd)
                        sums.append(total + pltpu.roll(total, BLK, 1))
                    results.append(
                        [jnp.where(left, sums[2 * duo], sums[2 * duo + 1]) for duo in range(NF // 2)]
                    )
                for duo in range(NF // 2):
                    out_ref[rows, duo * LANES : (duo + 1) * LANES] = jnp.concatenate(
                        [results[0][duo], results[1][duo]], 0
                    ).astype(BF16)
            return carry

        lax.fori_loop(0, parts, lists, 0)

    for block in range(count):
        store(block).wait()


def outgoing(section, atmos, length, ids, owned, blocks, ops, weights, state, coef, swept):
    lists, halves, cap, square = weights.shape
    slots = lists * halves * cap
    count, width = blocks.shape
    padded = -(-count // LANES) * LANES
    levels = state.shape[0]
    whole = pl.BlockSpec(memory_space=pltpu.VMEM)
    there = pl.BlockSpec(memory_space=pl.ANY)
    held = pltpu.VMEM((SECOND - FIRST, levels, WIDTH), BF16)
    return pl.pallas_call(
        outgoing_kernel,
        out_shape=(
            jax.ShapeDtypeStruct((slots, width), BF16),
            jax.ShapeDtypeStruct((slots // LANES, LANES), F32),
            jax.ShapeDtypeStruct((1, padded), F32),
            pltpu.HBM(swept.shape, BF16),
        ),
        in_specs=[pl.BlockSpec(memory_space=pltpu.SMEM)] + [whole] * 6 + [there] * 4,
        out_specs=(whole, whole, whole, there),
        input_output_aliases={10: 3},
        scratch_shapes=[
            pltpu.VMEM((slots, width), F32),
            pltpu.VMEM(weights.shape, BF16),
            held,
            held,
            held,
            pltpu.SemaphoreType.DMA((lists // GROUP,)),
            pltpu.SemaphoreType.DMA((3, SECOND - FIRST)),
        ],
        compiler_params=pltpu.CompilerParams(vmem_limit_bytes=32 << 20),
        name="outgoing",
    )(section, atmos, length, ids, owned, blocks, ops, weights, state, coef, swept)


def early_kernel(ops_ref, state_ref, coef_ref, swept_hbm, out_ref):
    out_ref[...] = advance(ops_ref, state_ref[...], coef_ref[...])


def early_sweep(ops, state, coef, swept, start, stop):
    levels, cells = state.shape
    columns = pl.BlockSpec((levels, WIDTH), lambda i: (0, early_column(i + start)))
    there = pl.BlockSpec(memory_space=pl.ANY)
    return pl.pallas_call(
        early_kernel,
        grid=(stop - start,),
        out_shape=pltpu.HBM(swept.shape, BF16),
        in_specs=[pl.BlockSpec(ops.shape, lambda i: (0, 0, 0)), columns, columns, there],
        out_specs=pl.BlockSpec((levels, WIDTH), lambda i: (0, i + start)),
        input_output_aliases={3: 0},
        compiler_params=pltpu.CompilerParams(vmem_limit_bytes=16 << 20),
        name="early",
    )(ops, state, coef, swept)


def backward_lists(arrived_ref, weights_hbm, weights, terms, weight_sems):
    lane = lax.broadcasted_iota(jnp.int32, (8, LANES), 1)
    row = lax.broadcasted_iota(jnp.int32, (8, LANES), 0)
    left = lane < BLK
    source = (((lane >> 1) & 15) << 3) + row
    half_kind = ((lane >> 5) & 1) * 2 + (lane & 1)

    def lists(part, carry):
        fetch_weights(weights_hbm, weights, weight_sems, part).wait()
        for inner in range(GROUP):
            tile = part * GROUP + inner
            rows = pl.ds(pl.multiple_of(tile * 16, 16), 16)
            echoes = arrived_ref[rows, :].astype(F32)
            results = []
            for half in range(2):
                lines = []
                for duo in range(NF // 2):
                    both = echoes[half * 8 : half * 8 + 8, duo * LANES : (duo + 1) * LANES]
                    turned = pltpu.roll(both, BLK, 1)
                    lines += [
                        jnp.where(left, both, 0.0),
                        jnp.where(left, 0.0, turned),
                        jnp.where(left, turned, 0.0),
                        jnp.where(left, 0.0, both),
                    ]
                product = lax.dot_general(
                    jnp.concatenate(lines, 0).astype(BF16),
                    half_list(weights, tile, half),
                    (((1,), (1,)), ((), ())),
                    preferred_element_type=F32,
                )
                outs = []
                for duo in range(NF // 2):
                    fields = []
                    for field in (2 * duo, 2 * duo + 1):
                        total = None
                        for side in range(2):
                            for parity in range(2):
                                start = field * 16 + parity * 8
                                value = pick(
                                    product[start : start + 8, side * LANES : (side + 1) * LANES],
                                    source,
                                )
                                kind = side * 2 + parity
                                total = (
                                    value
                                    if total is None
                                    else jnp.where(half_kind == kind, value, total)
                                )
                        fields.append(total)
                    outs.append(jnp.where(left, fields[0], fields[1]))
                results.append(outs)
            for duo in range(NF // 2):
                terms[rows, duo * LANES : (duo + 1) * LANES] = jnp.concatenate(
                    [results[0][duo], results[1][duo]], 0
                ).astype(BF16)
        return carry

    lax.fori_loop(0, weights.shape[0] // GROUP, lists, 0)


def sum_terms(key_ref, table_ref, terms, forcing):
    slots = terms.shape[0]
    pairs = forcing.shape[0] // 8
    table = jnp.broadcast_to(table_ref[...], (LANES, table_ref.shape[1])).T[: 2 * pairs]
    picks = [
        jnp.where(table == key_ref[r : r + 1, :], 1.0, 0.0).astype(BF16)
        for r in range(slots // LANES)
    ]
    total = jnp.dot(jnp.concatenate(picks, 1), terms[...], preferred_element_type=F32)
    left = lanes_below((pairs, LANES), BLK)
    for duo in range(NF // 2):
        even = total[:pairs, duo * LANES : (duo + 1) * LANES]
        odd = total[pairs:, duo * LANES : (duo + 1) * LANES]
        fields = (
            jnp.where(left, even, pltpu.roll(odd, BLK, 1)),
            jnp.where(left, pltpu.roll(even, BLK, 1), odd),
        )
        for n, field in enumerate(fields):
            coarse = field.astype(BF16).astype(F32)
            forcing[pl.ds(2 * duo + n, pairs, stride=8), :] = coarse
            forcing[pl.ds(NF + 2 * duo + n, pairs, stride=8), :] = field - coarse


def late_kernel(
    section_ref,
    key_ref,
    table_ref,
    arrived_ref,
    weights_hbm,
    write_ref,
    ops_ref,
    swept_ref,
    state_ref,
    coef_ref,
    out_hbm,
    terms,
    forcing,
    early,
    last,
    weights,
    weight_sems,
    sems,
):
    step = pl.program_id(0)
    backward = jnp.logical_and(step == 0, section_ref[0] == 0)

    @pl.when(backward)
    def _():
        for part in range(weight_sems.shape[0]):
            fetch_weights(weights_hbm, weights, weight_sems, part).start()

    slot = step % 2
    span = 3 * WIDTH
    ready = pltpu.make_async_copy(
        early.at[slot],
        out_hbm.at[:, pl.ds(pl.multiple_of(step * span, span), 2 * WIDTH)],
        sems.at[slot],
    )
    swept = pltpu.make_async_copy(
        last.at[slot],
        out_hbm.at[:, pl.ds(pl.multiple_of(step * span + 2 * WIDTH, WIDTH), WIDTH)],
        sems.at[2 + slot],
    )
    before = 1 - slot
    ready_before = pltpu.make_async_copy(
        early.at[before], out_hbm.at[:, pl.ds(0, 2 * WIDTH)], sems.at[before]
    )
    swept_before = pltpu.make_async_copy(
        last.at[before], out_hbm.at[:, pl.ds(0, WIDTH)], sems.at[2 + before]
    )

    last[slot] = advance(ops_ref, state_ref[...], coef_ref[...])

    @pl.when(backward)
    def _():
        backward_lists(arrived_ref, weights_hbm, weights, terms, weight_sems)

    @pl.when(step == 0)
    def _():
        @pl.when(section_ref[0] == 1)
        def _():
            terms[...] = arrived_ref[...]

        sum_terms(key_ref, table_ref, terms, forcing)

    write = write_ref[...]
    coarse = write.astype(BF16).astype(F32)
    fine = write - coarse
    factor = jnp.concatenate([coarse, coarse, fine, fine], 0).astype(BF16)

    def added(start, width):
        base = step * (span // LANES) + start // LANES
        fields = jnp.concatenate(
            [
                forcing[pl.ds(pl.multiple_of((base + t) * 8, 8), 8), :]
                for t in range(width // LANES)
            ],
            1,
        )
        operand = jnp.concatenate([fields, fields], 0).astype(BF16)
        return lax.dot_general(
            factor, operand, (((0,), (0,)), ((), ())), preferred_element_type=F32
        )

    early[slot] = (swept_ref[...].astype(F32) + added(0, 2 * WIDTH)).astype(BF16)
    ready.start()
    last[slot] = (last[slot].astype(F32) + added(2 * WIDTH, WIDTH)).astype(BF16)
    swept.start()

    @pl.when(step > 0)
    def _():
        ready_before.wait()
        swept_before.wait()

    @pl.when(step == pl.num_programs(0) - 1)
    def _():
        ready.wait()
        swept.wait()


def late(section, key, table, arrived, weights, write, ops, swept, state, coef):
    levels, cells = state.shape
    slots, width = arrived.shape
    whole = pl.BlockSpec(memory_space=pltpu.VMEM)
    columns = pl.BlockSpec((levels, WIDTH), lambda i: (0, 3 * i + 2))
    return pl.pallas_call(
        late_kernel,
        grid=(cells // (3 * WIDTH),),
        out_shape=jax.ShapeDtypeStruct((levels, cells), BF16),
        in_specs=[
            pl.BlockSpec(memory_space=pltpu.SMEM),
            whole,
            whole,
            whole,
            pl.BlockSpec(memory_space=pl.ANY),
            whole,
            whole,
            pl.BlockSpec((levels, 2 * WIDTH), lambda i: (0, i)),
            columns,
            columns,
        ],
        out_specs=pl.BlockSpec(memory_space=pl.ANY),
        scratch_shapes=[
            pltpu.VMEM((slots, width), BF16),
            pltpu.VMEM((cells // LANES * 8, LANES), F32),
            pltpu.VMEM((2, levels, 2 * WIDTH), BF16),
            pltpu.VMEM((2, levels, WIDTH), BF16),
            pltpu.VMEM(weights.shape, BF16),
            pltpu.SemaphoreType.DMA((weights.shape[0] // GROUP,)),
            pltpu.SemaphoreType.DMA((4,)),
        ],
        compiler_params=pltpu.CompilerParams(vmem_limit_bytes=36 << 20),
        name="late",
    )(section, key, table, arrived, weights, write, ops, swept, state, coef)


def body(
    adjoint_state,
    tangent_coef,
    column_ops,
    surf_read,
    surf_write,
    remap_weights,
    pair_atmos,
    pair_ocean,
    list_len,
    ocean_owned,
):
    section = lax.axis_index("sec")
    lists, cap = pair_atmos.shape[1:]
    state = pltpu.with_memory_space_constraint(adjoint_state[0], pltpu.HBM)
    coef = pltpu.with_memory_space_constraint(tangent_coef[0], pltpu.HBM)
    weights = pltpu.with_memory_space_constraint(
        remap_weights[0].reshape(lists, cap // 8, 8, BLK * BLK), pltpu.HBM
    )
    ops = column_ops[0].transpose(0, 2, 1)
    which = section.reshape(1).astype(jnp.int32)
    arrived_ids = lax.all_to_all(pair_ocean[0], "tile", split_axis=0, concat_axis=0, tiled=True)
    surface, swept = surface_blocks(surf_read[0], ops, state, coef)
    partner = lax.ppermute(surface, "sec", [(0, 1), (1, 0)])
    swept = early_sweep(ops, state, coef, swept, 1, FIRST)
    payload, in_key, in_table, swept = outgoing(
        which,
        pair_atmos[0].T,
        list_len,
        arrived_ids.reshape(lists, 1, cap),
        ocean_owned,
        partner,
        ops,
        weights,
        state,
        coef,
        swept,
    )
    received = lax.all_to_all(
        payload.reshape(lists, cap, NF * BLK), "tile", split_axis=0, concat_axis=0, tiled=True
    )
    swept = early_sweep(ops, state, coef, swept, SECOND, 6)
    swept = pltpu.with_memory_space_constraint(swept, pltpu.HBM)
    arrived = received.reshape(lists * cap, NF * BLK)
    write = surf_write[0].T
    out = late(which, in_key, in_table, arrived, weights, write, ops, swept, state, coef)
    return out[None]


def solution(mesh):
    in_specs = (
        P("sec", None, "tile"),
        P("sec", None, "tile"),
        P("sec", None, None, None),
        P("sec", None, None),
        P("sec", None, None),
        P("tile", None, None, None),
        P("tile", None, None),
        P("tile", None, None),
        P("tile", None),
        P("tile", None),
    )
    out_specs = P("sec", None, "tile")
    return jax.shard_map(body, mesh=mesh, in_specs=in_specs, out_specs=out_specs, check_vma=False)
```

```python
import jax
import jax.numpy as jnp
from jax import lax
from jax.experimental import pallas as pl
from jax.experimental.pallas import tpu as pltpu
from jax.sharding import PartitionSpec as P

NF = 4
BLK = 64
NSTEP = 16
LANES = 128
GROUP = 8
MANY = 2
WIDTH = 4096
FIRST = 2
SECOND = 3
BF16 = jnp.bfloat16
F32 = jnp.float32


def lanes_below(shape, edge):
    return lax.broadcasted_iota(jnp.int32, shape, len(shape) - 1) < edge


def advance(ops_ref, current, coef):
    factors = coef.astype(F32)
    for step in range(NSTEP):
        stepped = jnp.dot(ops_ref[step], current, preferred_element_type=F32)
        current = (stepped * factors).astype(BF16)
    return current


def early_column(block):
    return block // 2 * 3 + block % 2


def surface_kernel(
    read_ref, ops_ref, state_hbm, coef_hbm, out_ref, swept_hbm, state, coef, swept, held, sems
):
    parts = sems.shape[0] - 2
    tiles = WIDTH // LANES

    def columns(part):
        return pl.ds(pl.multiple_of(part * WIDTH, WIDTH), WIDTH)

    def fetch(part):
        return pltpu.make_async_copy(
            state_hbm.at[:, columns(part)], state.at[:, columns(part)], sems.at[part]
        )

    factors = pltpu.make_async_copy(coef_hbm.at[:, pl.ds(0, WIDTH)], coef, sems.at[parts])
    store = pltpu.make_async_copy(swept, swept_hbm.at[:, pl.ds(0, WIDTH)], sems.at[parts + 1])
    fetch(0).start()
    factors.start()
    for part in range(1, parts):
        fetch(part).start()

    def compute(part):
        fields = jnp.dot(read_ref[...], state[:, columns(part)], preferred_element_type=F32)
        for tile in range(tiles):
            row = pl.multiple_of((part * tiles + tile) * 8, 8)
            held[pl.ds(row, NF), :] = fields[:, tile * LANES : (tile + 1) * LANES]

    fetch(0).wait()
    factors.wait()
    swept[...] = advance(ops_ref, state[:, :WIDTH], coef[...])
    store.start()
    compute(0)

    def following(part, carry):
        fetch(part).wait()
        compute(part)
        return carry

    lax.fori_loop(1, parts, following, 0)
    pairs = out_ref.shape[0] // 2
    left = lanes_below((pairs, LANES), BLK)
    for duo in range(NF // 2):
        first = held[pl.ds(2 * duo, pairs, stride=8), :]
        second = held[pl.ds(2 * duo + 1, pairs, stride=8), :]
        cols = slice(duo * LANES, (duo + 1) * LANES)
        even = jnp.where(left, first, pltpu.roll(second, BLK, 1))
        odd = jnp.where(left, pltpu.roll(first, BLK, 1), second)
        out_ref[:pairs, cols] = even.astype(BF16)
        out_ref[pairs:, cols] = odd.astype(BF16)
    store.wait()


def surface_blocks(read, ops, state, coef):
    levels, cells = state.shape
    blocks = cells // BLK
    parts = cells // WIDTH
    whole = pl.BlockSpec(memory_space=pltpu.VMEM)
    there = pl.BlockSpec(memory_space=pl.ANY)
    return pl.pallas_call(
        surface_kernel,
        out_shape=(
            jax.ShapeDtypeStruct((blocks, NF * BLK), BF16),
            pltpu.HBM((levels, cells // 3 * 2), BF16),
        ),
        in_specs=[whole, whole, there, there],
        out_specs=(whole, there),
        scratch_shapes=[
            pltpu.VMEM((levels, cells), BF16),
            pltpu.VMEM((levels, WIDTH), BF16),
            pltpu.VMEM((levels, WIDTH), BF16),
            pltpu.VMEM((blocks // 2 * 8, LANES), F32),
            pltpu.SemaphoreType.DMA((parts + 2,)),
        ],
        compiler_params=pltpu.CompilerParams(vmem_limit_bytes=24 << 20),
        name="surface",
    )(read, ops, state, coef)


def fetch_weights(weights_hbm, weights, sems, part):
    lists = pl.ds(part * GROUP, GROUP)
    return pltpu.make_async_copy(weights_hbm.at[lists], weights.at[lists], sems.at[part])


def half_list(weights, tile, half):
    return jnp.concatenate(
        [weights[tile, half, :, q * LANES : (q + 1) * LANES] for q in range(BLK // 2)], 0
    )


def fill_spread(spread):
    row = lax.broadcasted_iota(jnp.int32, spread.shape, 0)
    col = lax.broadcasted_iota(jnp.int32, spread.shape, 1)
    source = (col >> 9) * BLK + ((col >> 3) & 31) * 2 + ((col >> 8) & 1)
    spread[...] = jnp.where(row == source, 1.0, 0.0).astype(BF16)


def own_slot(rows, cols):
    row = lax.broadcasted_iota(jnp.int32, (rows, cols), 0)
    col = lax.broadcasted_iota(jnp.int32, (rows, cols), 1)
    return (row & 7) == (col & 7)


def pick(values, lanes):
    return jnp.take_along_axis(values, lanes, axis=1, mode="promise_in_bounds")


def widened(values):
    rows, cols = values.shape
    return jnp.concatenate([values, jnp.zeros((rows, LANES - cols), values.dtype)], 1)


def slot_rows(values):
    lists = values.shape[0]
    lane = lax.broadcasted_iota(jnp.int32, (lists, LANES), 1)
    row = lax.broadcasted_iota(jnp.int32, (lists, LANES), 0)
    spread = jnp.where((lane >> 4) == (row & 7), pick(widened(values), lane & 15), 0.0)
    return jnp.sum(spread.reshape(lists // 8, 8, LANES), 1)


def even_first(values, padded):
    count = values.shape[1]
    pairs = count // 2
    lane = lax.broadcasted_iota(jnp.int32, (8, LANES), 1)
    sources = []
    for start in range(0, count, LANES):
        source = values[:, start : min(start + LANES, count)]
        sources.append(source if source.shape[1] == LANES else widened(source))
    sources = [jnp.broadcast_to(source, (8, LANES)) for source in sources]
    tiles = []
    for tile in range(padded // LANES):
        spots = [
            2 * j if j < pairs else 2 * (j - pairs) + 1
            for j in range(tile * LANES, min((tile + 1) * LANES, count))
        ]
        at = tile * LANES + lane
        wanted = jnp.where(at < pairs, 2 * at, 2 * (at - pairs) + 1)
        result = jnp.full((8, LANES), -2.0, F32)
        for index in sorted({spot // LANES for spot in spots}):
            inside = ((wanted >> 7) == index) & (at < count)
            result = jnp.where(inside, pick(sources[index], wanted & 127), result)
        tiles.append(result)
    return jnp.concatenate(tiles, 1)[:1]


def outgoing_kernel(
    section_ref,
    atmos_ref,
    length_ref,
    ids_ref,
    owned_ref,
    blocks_ref,
    ops_ref,
    weights_hbm,
    state_hbm,
    coef_hbm,
    swept_in,
    out_ref,
    in_key_ref,
    in_table_ref,
    swept_hbm,
    chosen,
    spread,
    wide,
    weights,
    state,
    coef,
    swept,
    weight_sems,
    sems,
):
    count = state.shape[0]

    def fetch(block):
        columns = pl.ds(pl.multiple_of(early_column(FIRST + block) * WIDTH, WIDTH), WIDTH)
        return (
            pltpu.make_async_copy(state_hbm.at[:, columns], state.at[block], sems.at[0, block]),
            pltpu.make_async_copy(coef_hbm.at[:, columns], coef.at[block], sems.at[1, block]),
        )

    def store(block):
        columns = pl.ds(pl.multiple_of((FIRST + block) * WIDTH, WIDTH), WIDTH)
        return pltpu.make_async_copy(
            swept.at[block], swept_hbm.at[:, columns], sems.at[2, block]
        )

    for block in range(count):
        for copy in fetch(block):
            copy.start()

    @pl.when(section_ref[0] == 1)
    def _():
        for part in range(weight_sems.shape[0]):
            fetch_weights(weights_hbm, weights, weight_sems, part).start()

    def sweep_block(block, carry):
        for copy in fetch(block):
            copy.wait()
        swept[block] = advance(ops_ref, state[block], coef[block])
        store(block).start()
        return carry

    lax.fori_loop(0, count, sweep_block, 0)
    blocks = blocks_ref.shape[0]
    pairs = blocks // 2
    padded = in_table_ref.shape[1]
    parts = in_key_ref.shape[0]
    first = section_ref[0] == 0
    lane = lax.broadcasted_iota(jnp.int32, (8, LANES), 1)
    row = lax.broadcasted_iota(jnp.int32, (8, LANES), 0)
    lengths = jnp.broadcast_to(widened(length_ref[...].astype(F32)), (8, LANES))
    live = (lane & 15).astype(F32) < pick(lengths, row * 8 + (lane >> 4))
    atmos = atmos_ref[...]
    atmos = ((atmos & 1) * pairs + (atmos >> 1)).astype(F32)
    atmos_key = jnp.where(live, slot_rows(widened(atmos).T[: atmos.shape[1]]), -1.0)
    ocean_key = slot_rows(ids_ref[:, 0, :].astype(F32))
    owned_table = even_first(owned_ref[...].astype(F32), padded)
    plain_table = lax.broadcasted_iota(jnp.int32, (1, padded), 1).astype(F32)
    out_key = jnp.where(first, ocean_key, atmos_key)
    out_table = jnp.where(first, owned_table, plain_table)
    in_key_ref[...] = jnp.where(first, atmos_key, ocean_key)
    in_table_ref[...] = jnp.where(first, plain_table, owned_table)

    for part in range(parts):
        key = jnp.broadcast_to(out_key[part : part + 1, :], (LANES, LANES)).T
        pieces = []
        for start in range(0, blocks, LANES):
            stop = min(start + LANES, blocks)
            piece = jnp.where(key == out_table[:, start : start + LANES], 1.0, 0.0).astype(BF16)
            pieces.append(piece[:, : stop - start])
        chosen[part * LANES : (part + 1) * LANES, :] = jnp.dot(
            jnp.concatenate(pieces, 1), blocks_ref[...], preferred_element_type=F32
        )

    @pl.when(first)
    def _():
        out_ref[...] = chosen[...].astype(BF16)

    @pl.when(jnp.logical_not(first))
    def _():
        fill_spread(spread)
        left = lane < BLK
        mine = own_slot(MANY * LANES, 2 * LANES)

        def lists(part, carry):
            span = MANY * LANES
            here = pl.ds(pl.multiple_of(part * span, span), span)
            for duo in range(NF // 2):
                values = chosen[here, duo * LANES : (duo + 1) * LANES].astype(BF16)
                for chunk in range(4):
                    cols = slice(chunk * 2 * LANES, (chunk + 1) * 2 * LANES)
                    spaced = jnp.dot(values, spread[:, cols], preferred_element_type=F32)
                    wide[:, (duo * 4 + chunk) * 2 * LANES : (duo * 4 + chunk + 1) * 2 * LANES] = (
                        jnp.where(mine, spaced, 0.0)
                    )
            for piece in range(MANY):
                fetch_weights(weights_hbm, weights, weight_sems, part * MANY + piece).wait()
            for inner in range(MANY * GROUP):
                tile = part * MANY * GROUP + inner
                rows = pl.ds(pl.multiple_of(tile * 16, 16), 16)
                results = []
                for half in range(2):
                    start = inner * 16 + half * 8
                    lines = [
                        wide[start : start + 8, line * 2 * LANES : (line + 1) * 2 * LANES]
                        for line in range(2 * NF)
                    ]
                    product = jnp.dot(
                        jnp.concatenate(lines, 0).astype(BF16),
                        half_list(weights, tile, half),
                        preferred_element_type=F32,
                    )
                    sums = []
                    for field in range(NF):
                        even = product[field * 16 : field * 16 + 8]
                        odd = product[field * 16 + 8 : field * 16 + 16]
                        total = jnp.where(left, even, odd)
                        sums.append(total + pltpu.roll(total, BLK, 1))
                    results.append(
                        [jnp.where(left, sums[2 * duo], sums[2 * duo + 1]) for duo in range(NF // 2)]
                    )
                for duo in range(NF // 2):
                    out_ref[rows, duo * LANES : (duo + 1) * LANES] = jnp.concatenate(
                        [results[0][duo], results[1][duo]], 0
                    ).astype(BF16)
            return carry

        lax.fori_loop(0, parts // MANY, lists, 0)

    for block in range(count):
        store(block).wait()


def outgoing(section, atmos, length, ids, owned, blocks, ops, weights, state, coef, swept):
    lists, halves, cap, _ = weights.shape
    slots = lists * halves * cap
    count, width = blocks.shape
    padded = -(-count // LANES) * LANES
    levels = state.shape[0]
    whole = pl.BlockSpec(memory_space=pltpu.VMEM)
    there = pl.BlockSpec(memory_space=pl.ANY)
    held = pltpu.VMEM((SECOND - FIRST, levels, WIDTH), BF16)
    return pl.pallas_call(
        outgoing_kernel,
        out_shape=(
            jax.ShapeDtypeStruct((slots, width), BF16),
            jax.ShapeDtypeStruct((slots // LANES, LANES), F32),
            jax.ShapeDtypeStruct((1, padded), F32),
            pltpu.HBM(swept.shape, BF16),
        ),
        in_specs=[pl.BlockSpec(memory_space=pltpu.SMEM)] + [whole] * 6 + [there] * 4,
        out_specs=(whole, whole, whole, there),
        input_output_aliases={10: 3},
        scratch_shapes=[
            pltpu.VMEM((slots, width), F32),
            pltpu.VMEM((LANES, 8 * LANES), BF16),
            pltpu.VMEM((MANY * LANES, 16 * LANES), F32),
            pltpu.VMEM(weights.shape, BF16),
            held,
            held,
            held,
            pltpu.SemaphoreType.DMA((lists // GROUP,)),
            pltpu.SemaphoreType.DMA((3, SECOND - FIRST)),
        ],
        compiler_params=pltpu.CompilerParams(vmem_limit_bytes=32 << 20),
        name="outgoing",
    )(section, atmos, length, ids, owned, blocks, ops, weights, state, coef, swept)


def early_kernel(ops_ref, state_ref, coef_ref, swept_hbm, out_ref):
    out_ref[...] = advance(ops_ref, state_ref[...], coef_ref[...])


def early_sweep(ops, state, coef, swept, start, stop):
    levels, _ = state.shape
    columns = pl.BlockSpec((levels, WIDTH), lambda i: (0, early_column(i + start)))
    there = pl.BlockSpec(memory_space=pl.ANY)
    return pl.pallas_call(
        early_kernel,
        grid=(stop - start,),
        out_shape=pltpu.HBM(swept.shape, BF16),
        in_specs=[pl.BlockSpec(ops.shape, lambda i: (0, 0, 0)), columns, columns, there],
        out_specs=pl.BlockSpec((levels, WIDTH), lambda i: (0, i + start)),
        input_output_aliases={3: 0},
        compiler_params=pltpu.CompilerParams(vmem_limit_bytes=16 << 20),
        name="early",
    )(ops, state, coef, swept)


def backward_lists(arrived_ref, weights_hbm, weights, terms, spread, wide, weight_sems):
    left = lanes_below((8, LANES), BLK)
    mine = own_slot(8, 2 * LANES)
    fill_spread(spread)

    def lists(part, carry):
        for piece in range(MANY):
            fetch_weights(weights_hbm, weights, weight_sems, part * MANY + piece).wait()
        for inner in range(MANY * GROUP):
            tile = part * MANY * GROUP + inner
            echoes = arrived_ref[pl.ds(pl.multiple_of(tile * 16, 16), 16), :].astype(F32)
            for half in range(2):
                lines = []
                for duo in range(NF // 2):
                    both = echoes[half * 8 : half * 8 + 8, duo * LANES : (duo + 1) * LANES]
                    turned = pltpu.roll(both, BLK, 1)
                    lines += [
                        jnp.where(left, both, 0.0),
                        jnp.where(left, 0.0, turned),
                        jnp.where(left, turned, 0.0),
                        jnp.where(left, 0.0, both),
                    ]
                product = lax.dot_general(
                    jnp.concatenate(lines, 0).astype(BF16),
                    half_list(weights, tile, half),
                    (((1,), (1,)), ((), ())),
                    preferred_element_type=F32,
                )
                start = inner * 16 + half * 8
                for line in range(2 * NF):
                    wide[start : start + 8, line * 2 * LANES : (line + 1) * 2 * LANES] = jnp.where(
                        mine, product[line * 8 : line * 8 + 8], 0.0
                    )
        span = MANY * LANES
        here = pl.ds(pl.multiple_of(part * span, span), span)
        for duo in range(NF // 2):
            terms[here, duo * LANES : (duo + 1) * LANES] = lax.dot_general(
                wide[:, duo * 8 * LANES : (duo + 1) * 8 * LANES].astype(BF16),
                spread[...],
                (((1,), (1,)), ((), ())),
                preferred_element_type=F32,
            ).astype(BF16)
        return carry

    lax.fori_loop(0, weights.shape[0] // GROUP // MANY, lists, 0)


def sum_terms(key_ref, table_ref, terms, forcing):
    slots = terms.shape[0]
    pairs = forcing.shape[0] // 8
    table = jnp.broadcast_to(table_ref[...], (LANES, table_ref.shape[1])).T[: 2 * pairs]
    picks = [
        jnp.where(table == key_ref[r : r + 1, :], 1.0, 0.0).astype(BF16)
        for r in range(slots // LANES)
    ]
    total = jnp.dot(jnp.concatenate(picks, 1), terms[...], preferred_element_type=F32)
    left = lanes_below((pairs, LANES), BLK)
    for duo in range(NF // 2):
        even = total[:pairs, duo * LANES : (duo + 1) * LANES]
        odd = total[pairs:, duo * LANES : (duo + 1) * LANES]
        fields = (
            jnp.where(left, even, pltpu.roll(odd, BLK, 1)),
            jnp.where(left, pltpu.roll(even, BLK, 1), odd),
        )
        for n, field in enumerate(fields):
            coarse = field.astype(BF16).astype(F32)
            forcing[pl.ds(2 * duo + n, pairs, stride=8), :] = coarse
            forcing[pl.ds(NF + 2 * duo + n, pairs, stride=8), :] = field - coarse


def late_kernel(
    section_ref,
    key_ref,
    table_ref,
    arrived_ref,
    weights_hbm,
    write_ref,
    ops_ref,
    swept_ref,
    state_ref,
    coef_ref,
    out_hbm,
    terms,
    forcing,
    early,
    last,
    spread,
    wide,
    weights,
    weight_sems,
    sems,
):
    step = pl.program_id(0)
    backward = jnp.logical_and(step == 0, section_ref[0] == 0)

    @pl.when(backward)
    def _():
        for part in range(weight_sems.shape[0]):
            fetch_weights(weights_hbm, weights, weight_sems, part).start()

    slot = step % 2
    span = 3 * WIDTH
    ready = pltpu.make_async_copy(
        early.at[slot],
        out_hbm.at[:, pl.ds(pl.multiple_of(step * span, span), 2 * WIDTH)],
        sems.at[slot],
    )
    swept = pltpu.make_async_copy(
        last.at[slot],
        out_hbm.at[:, pl.ds(pl.multiple_of(step * span + 2 * WIDTH, WIDTH), WIDTH)],
        sems.at[2 + slot],
    )
    before = 1 - slot
    ready_before = pltpu.make_async_copy(
        early.at[before], out_hbm.at[:, pl.ds(0, 2 * WIDTH)], sems.at[before]
    )
    swept_before = pltpu.make_async_copy(
        last.at[before], out_hbm.at[:, pl.ds(0, WIDTH)], sems.at[2 + before]
    )

    last[slot] = advance(ops_ref, state_ref[...], coef_ref[...])

    @pl.when(backward)
    def _():
        backward_lists(arrived_ref, weights_hbm, weights, terms, spread, wide, weight_sems)

    @pl.when(step == 0)
    def _():
        @pl.when(section_ref[0] == 1)
        def _():
            terms[...] = arrived_ref[...]

        sum_terms(key_ref, table_ref, terms, forcing)

    write = write_ref[...]
    coarse = write.astype(BF16).astype(F32)
    fine = write - coarse
    factor = jnp.concatenate([coarse, coarse, fine, fine], 0).astype(BF16)

    def added(start, width):
        base = step * (span // LANES) + start // LANES
        fields = jnp.concatenate(
            [
                forcing[pl.ds(pl.multiple_of((base + t) * 8, 8), 8), :]
                for t in range(width // LANES)
            ],
            1,
        )
        operand = jnp.concatenate([fields, fields], 0).astype(BF16)
        return lax.dot_general(
            factor, operand, (((0,), (0,)), ((), ())), preferred_element_type=F32
        )

    early[slot] = (swept_ref[...].astype(F32) + added(0, 2 * WIDTH)).astype(BF16)
    ready.start()
    last[slot] = (last[slot].astype(F32) + added(2 * WIDTH, WIDTH)).astype(BF16)
    swept.start()

    @pl.when(step > 0)
    def _():
        ready_before.wait()
        swept_before.wait()

    @pl.when(step == pl.num_programs(0) - 1)
    def _():
        ready.wait()
        swept.wait()


def late(section, key, table, arrived, weights, write, ops, swept, state, coef):
    levels, cells = state.shape
    slots, width = arrived.shape
    whole = pl.BlockSpec(memory_space=pltpu.VMEM)
    columns = pl.BlockSpec((levels, WIDTH), lambda i: (0, 3 * i + 2))
    return pl.pallas_call(
        late_kernel,
        grid=(cells // (3 * WIDTH),),
        out_shape=jax.ShapeDtypeStruct((levels, cells), BF16),
        in_specs=[
            pl.BlockSpec(memory_space=pltpu.SMEM),
            whole,
            whole,
            whole,
            pl.BlockSpec(memory_space=pl.ANY),
            whole,
            whole,
            pl.BlockSpec((levels, 2 * WIDTH), lambda i: (0, i)),
            columns,
            columns,
        ],
        out_specs=pl.BlockSpec(memory_space=pl.ANY),
        scratch_shapes=[
            pltpu.VMEM((slots, width), BF16),
            pltpu.VMEM((cells // LANES * 8, LANES), F32),
            pltpu.VMEM((2, levels, 2 * WIDTH), BF16),
            pltpu.VMEM((2, levels, WIDTH), BF16),
            pltpu.VMEM((LANES, 8 * LANES), BF16),
            pltpu.VMEM((MANY * LANES, 16 * LANES), F32),
            pltpu.VMEM(weights.shape, BF16),
            pltpu.SemaphoreType.DMA((weights.shape[0] // GROUP,)),
            pltpu.SemaphoreType.DMA((4,)),
        ],
        compiler_params=pltpu.CompilerParams(vmem_limit_bytes=36 << 20),
        name="late",
    )(section, key, table, arrived, weights, write, ops, swept, state, coef)


def body(
    adjoint_state,
    tangent_coef,
    column_ops,
    surf_read,
    surf_write,
    remap_weights,
    pair_atmos,
    pair_ocean,
    list_len,
    ocean_owned,
):
    section = lax.axis_index("sec")
    lists, cap = pair_atmos.shape[1:]
    state = pltpu.with_memory_space_constraint(adjoint_state[0], pltpu.HBM)
    coef = pltpu.with_memory_space_constraint(tangent_coef[0], pltpu.HBM)
    weights = pltpu.with_memory_space_constraint(
        remap_weights[0].reshape(lists, cap // 8, 8, BLK * BLK), pltpu.HBM
    )
    ops = column_ops[0].transpose(0, 2, 1)
    which = section.reshape(1).astype(jnp.int32)
    arrived_ids = lax.all_to_all(pair_ocean[0], "tile", split_axis=0, concat_axis=0, tiled=True)
    read = pltpu.with_memory_space_constraint(surf_read[0], pltpu.HBM)
    surface, swept = surface_blocks(read, ops, state, coef)
    partner = lax.ppermute(surface, "sec", [(0, 1), (1, 0)])
    swept = early_sweep(ops, state, coef, swept, 1, FIRST)
    payload, in_key, in_table, swept = outgoing(
        which,
        pair_atmos[0].T,
        list_len,
        arrived_ids.reshape(lists, 1, cap),
        ocean_owned,
        partner,
        ops,
        weights,
        state,
        coef,
        swept,
    )
    received = lax.all_to_all(
        payload.reshape(lists, cap, NF * BLK), "tile", split_axis=0, concat_axis=0, tiled=True
    )
    swept = early_sweep(ops, state, coef, swept, SECOND, 6)
    swept = pltpu.with_memory_space_constraint(swept, pltpu.HBM)
    arrived = received.reshape(lists * cap, NF * BLK)
    write = surf_write[0].T
    out = late(which, in_key, in_table, arrived, weights, write, ops, swept, state, coef)
    return out[None]


def solution(mesh):
    in_specs = (
        P("sec", None, "tile"),
        P("sec", None, "tile"),
        P("sec", None, None, None),
        P("sec", None, None),
        P("sec", None, None),
        P("tile", None, None, None),
        P("tile", None, None),
        P("tile", None, None),
        P("tile", None),
        P("tile", None),
    )
    out_specs = P("sec", None, "tile")
    return jax.shard_map(body, mesh=mesh, in_specs=in_specs, out_specs=out_specs, check_vma=False)
```

```python
import jax
import jax.numpy as jnp
from jax import lax
from jax.experimental import pallas as pl
from jax.experimental.pallas import tpu as pltpu
from jax.sharding import PartitionSpec as P

NF = 4
BLK = 64
NSTEP = 16
LANES = 128
GROUP = 8
MANY = 2
WIDTH = 4096
FIRST = 1
SECOND = 3
BF16 = jnp.bfloat16
F32 = jnp.float32


def lanes_below(shape, edge):
    return lax.broadcasted_iota(jnp.int32, shape, len(shape) - 1) < edge


def advance(ops_ref, current, coef):
    factors = coef.astype(F32)
    for step in range(NSTEP):
        stepped = lax.dot_general(
            ops_ref[step], current, (((0,), (0,)), ((), ())), preferred_element_type=F32
        )
        current = (stepped * factors).astype(BF16)
    return current


def early_column(block):
    return block // 2 * 3 + block % 2


def surface_kernel(
    read_ref, ops_ref, state_hbm, coef_hbm, out_ref, swept_hbm, state, coef, swept, held, sems
):
    parts = sems.shape[0] - 2
    tiles = WIDTH // LANES

    def columns(part):
        return pl.ds(pl.multiple_of(part * WIDTH, WIDTH), WIDTH)

    def fetch(part):
        return pltpu.make_async_copy(
            state_hbm.at[:, columns(part)], state.at[:, columns(part)], sems.at[part]
        )

    factors = pltpu.make_async_copy(coef_hbm.at[:, pl.ds(0, WIDTH)], coef, sems.at[parts])
    store = pltpu.make_async_copy(swept, swept_hbm.at[:, pl.ds(0, WIDTH)], sems.at[parts + 1])
    fetch(0).start()
    factors.start()
    for part in range(1, parts):
        fetch(part).start()

    def compute(part):
        fields = jnp.dot(read_ref[...], state[:, columns(part)], preferred_element_type=F32)
        for tile in range(tiles):
            row = pl.multiple_of((part * tiles + tile) * 8, 8)
            held[pl.ds(row, NF), :] = fields[:, tile * LANES : (tile + 1) * LANES]

    fetch(0).wait()
    factors.wait()
    swept[...] = advance(ops_ref, state[:, :WIDTH], coef[...])
    store.start()
    compute(0)

    def following(part, carry):
        fetch(part).wait()
        compute(part)
        return carry

    lax.fori_loop(1, parts, following, 0)
    pairs = out_ref.shape[0] // 2
    left = lanes_below((pairs, LANES), BLK)
    for duo in range(NF // 2):
        first = held[pl.ds(2 * duo, pairs, stride=8), :]
        second = held[pl.ds(2 * duo + 1, pairs, stride=8), :]
        cols = slice(duo * LANES, (duo + 1) * LANES)
        even = jnp.where(left, first, pltpu.roll(second, BLK, 1))
        odd = jnp.where(left, pltpu.roll(first, BLK, 1), second)
        out_ref[:pairs, cols] = even.astype(BF16)
        out_ref[pairs:, cols] = odd.astype(BF16)
    store.wait()


def surface_blocks(read, ops, state, coef):
    levels, cells = state.shape
    blocks = cells // BLK
    parts = cells // WIDTH
    whole = pl.BlockSpec(memory_space=pltpu.VMEM)
    there = pl.BlockSpec(memory_space=pl.ANY)
    return pl.pallas_call(
        surface_kernel,
        out_shape=(
            jax.ShapeDtypeStruct((blocks, NF * BLK), BF16),
            pltpu.HBM((levels, cells // 3 * 2), BF16),
        ),
        in_specs=[whole, whole, there, there],
        out_specs=(whole, there),
        scratch_shapes=[
            pltpu.VMEM((levels, cells), BF16),
            pltpu.VMEM((levels, WIDTH), BF16),
            pltpu.VMEM((levels, WIDTH), BF16),
            pltpu.VMEM((blocks // 2 * 8, LANES), F32),
            pltpu.SemaphoreType.DMA((parts + 2,)),
        ],
        compiler_params=pltpu.CompilerParams(vmem_limit_bytes=24 << 20),
        name="surface",
    )(read, ops, state, coef)


def fetch_weights(weights_hbm, weights, sems, part):
    lists = pl.ds(part * GROUP, GROUP)
    return pltpu.make_async_copy(weights_hbm.at[lists], weights.at[lists], sems.at[part])


def half_list(weights, tile, half):
    return jnp.concatenate(
        [weights[tile, half, :, q * LANES : (q + 1) * LANES] for q in range(BLK // 2)], 0
    )


def fill_spread(spread):
    row = lax.broadcasted_iota(jnp.int32, spread.shape, 0)
    col = lax.broadcasted_iota(jnp.int32, spread.shape, 1)
    source = (col >> 9) * BLK + ((col >> 3) & 31) * 2 + ((col >> 8) & 1)
    spread[...] = jnp.where(row == source, 1.0, 0.0).astype(BF16)


def own_slot(rows, cols):
    row = lax.broadcasted_iota(jnp.int32, (rows, cols), 0)
    col = lax.broadcasted_iota(jnp.int32, (rows, cols), 1)
    return (row & 7) == (col & 7)


def pick(values, lanes):
    return jnp.take_along_axis(values, lanes, axis=1, mode="promise_in_bounds")


def widened(values):
    rows, cols = values.shape
    return jnp.concatenate([values, jnp.zeros((rows, LANES - cols), values.dtype)], 1)


def slot_rows(values):
    lists = values.shape[0]
    lane = lax.broadcasted_iota(jnp.int32, (lists, LANES), 1)
    row = lax.broadcasted_iota(jnp.int32, (lists, LANES), 0)
    spread = jnp.where((lane >> 4) == (row & 7), pick(widened(values), lane & 15), 0.0)
    return jnp.sum(spread.reshape(lists // 8, 8, LANES), 1)


def even_first(values, padded):
    count = values.shape[1]
    pairs = count // 2
    lane = lax.broadcasted_iota(jnp.int32, (8, LANES), 1)
    sources = []
    for start in range(0, count, LANES):
        source = values[:, start : min(start + LANES, count)]
        sources.append(source if source.shape[1] == LANES else widened(source))
    sources = [jnp.broadcast_to(source, (8, LANES)) for source in sources]
    tiles = []
    for tile in range(padded // LANES):
        spots = [
            2 * j if j < pairs else 2 * (j - pairs) + 1
            for j in range(tile * LANES, min((tile + 1) * LANES, count))
        ]
        at = tile * LANES + lane
        wanted = jnp.where(at < pairs, 2 * at, 2 * (at - pairs) + 1)
        result = jnp.full((8, LANES), -2.0, F32)
        for index in sorted({spot // LANES for spot in spots}):
            inside = ((wanted >> 7) == index) & (at < count)
            result = jnp.where(inside, pick(sources[index], wanted & 127), result)
        tiles.append(result)
    return jnp.concatenate(tiles, 1)[:1]


def outgoing_kernel(
    section_ref,
    atmos_ref,
    length_ref,
    ids_ref,
    owned_ref,
    blocks_ref,
    ops_ref,
    weights_hbm,
    state_hbm,
    coef_hbm,
    swept_in,
    out_ref,
    in_key_ref,
    in_table_ref,
    swept_hbm,
    chosen,
    spread,
    wide,
    weights,
    state,
    coef,
    swept,
    weight_sems,
    sems,
):
    count = state.shape[0]

    def fetch(block):
        columns = pl.ds(pl.multiple_of(early_column(FIRST + block) * WIDTH, WIDTH), WIDTH)
        return (
            pltpu.make_async_copy(state_hbm.at[:, columns], state.at[block], sems.at[0, block]),
            pltpu.make_async_copy(coef_hbm.at[:, columns], coef.at[block], sems.at[1, block]),
        )

    def store(block):
        columns = pl.ds(pl.multiple_of((FIRST + block) * WIDTH, WIDTH), WIDTH)
        return pltpu.make_async_copy(
            swept.at[block], swept_hbm.at[:, columns], sems.at[2, block]
        )

    for block in range(count):
        for copy in fetch(block):
            copy.start()

    @pl.when(section_ref[0] == 1)
    def _():
        for part in range(weight_sems.shape[0]):
            fetch_weights(weights_hbm, weights, weight_sems, part).start()

    def sweep_block(block, carry):
        for copy in fetch(block):
            copy.wait()
        swept[block] = advance(ops_ref, state[block], coef[block])
        store(block).start()
        return carry

    lax.fori_loop(0, count, sweep_block, 0)
    blocks = blocks_ref.shape[0]
    pairs = blocks // 2
    padded = in_table_ref.shape[1]
    parts = in_key_ref.shape[0]
    first = section_ref[0] == 0
    lane = lax.broadcasted_iota(jnp.int32, (8, LANES), 1)
    row = lax.broadcasted_iota(jnp.int32, (8, LANES), 0)
    lengths = jnp.broadcast_to(widened(length_ref[...].astype(F32)), (8, LANES))
    live = (lane & 15).astype(F32) < pick(lengths, row * 8 + (lane >> 4))
    atmos = atmos_ref[...]
    atmos = ((atmos & 1) * pairs + (atmos >> 1)).astype(F32)
    atmos_key = jnp.where(live, slot_rows(widened(atmos).T[: atmos.shape[1]]), -1.0)
    ocean_key = slot_rows(ids_ref[:, 0, :].astype(F32))
    owned_table = even_first(owned_ref[...].astype(F32), padded)
    plain_table = lax.broadcasted_iota(jnp.int32, (1, padded), 1).astype(F32)
    out_key = jnp.where(first, ocean_key, atmos_key)
    out_table = jnp.where(first, owned_table, plain_table)
    in_key_ref[...] = jnp.where(first, atmos_key, ocean_key)
    in_table_ref[...] = jnp.where(first, plain_table, owned_table)

    for part in range(parts):
        key = jnp.broadcast_to(out_key[part : part + 1, :], (LANES, LANES)).T
        pieces = []
        for start in range(0, blocks, LANES):
            stop = min(start + LANES, blocks)
            piece = jnp.where(key == out_table[:, start : start + LANES], 1.0, 0.0).astype(BF16)
            pieces.append(piece[:, : stop - start])
        chosen[part * LANES : (part + 1) * LANES, :] = jnp.dot(
            jnp.concatenate(pieces, 1), blocks_ref[...], preferred_element_type=F32
        )

    @pl.when(first)
    def _():
        out_ref[...] = chosen[...].astype(BF16)

    @pl.when(jnp.logical_not(first))
    def _():
        fill_spread(spread)
        left = lane < BLK
        mine = own_slot(MANY * LANES, 2 * LANES)

        def lists(part, carry):
            span = MANY * LANES
            here = pl.ds(pl.multiple_of(part * span, span), span)
            for duo in range(NF // 2):
                values = chosen[here, duo * LANES : (duo + 1) * LANES].astype(BF16)
                for chunk in range(4):
                    cols = slice(chunk * 2 * LANES, (chunk + 1) * 2 * LANES)
                    spaced = jnp.dot(values, spread[:, cols], preferred_element_type=F32)
                    wide[:, (duo * 4 + chunk) * 2 * LANES : (duo * 4 + chunk + 1) * 2 * LANES] = (
                        jnp.where(mine, spaced, 0.0)
                    )
            for piece in range(MANY):
                fetch_weights(weights_hbm, weights, weight_sems, part * MANY + piece).wait()
            for inner in range(MANY * GROUP):
                tile = part * MANY * GROUP + inner
                rows = pl.ds(pl.multiple_of(tile * 16, 16), 16)
                results = []
                for half in range(2):
                    start = inner * 16 + half * 8
                    lines = [
                        wide[start : start + 8, line * 2 * LANES : (line + 1) * 2 * LANES]
                        for line in range(2 * NF)
                    ]
                    product = jnp.dot(
                        jnp.concatenate(lines, 0).astype(BF16),
                        half_list(weights, tile, half),
                        preferred_element_type=F32,
                    )
                    sums = []
                    for field in range(NF):
                        even = product[field * 16 : field * 16 + 8]
                        odd = product[field * 16 + 8 : field * 16 + 16]
                        total = jnp.where(left, even, odd)
                        sums.append(total + pltpu.roll(total, BLK, 1))
                    results.append(
                        [jnp.where(left, sums[2 * duo], sums[2 * duo + 1]) for duo in range(NF // 2)]
                    )
                for duo in range(NF // 2):
                    out_ref[rows, duo * LANES : (duo + 1) * LANES] = jnp.concatenate(
                        [results[0][duo], results[1][duo]], 0
                    ).astype(BF16)
            return carry

        lax.fori_loop(0, parts // MANY, lists, 0)

    for block in range(count):
        store(block).wait()


def outgoing(section, atmos, length, ids, owned, blocks, ops, weights, state, coef, swept):
    lists, halves, cap, _ = weights.shape
    slots = lists * halves * cap
    count, width = blocks.shape
    padded = -(-count // LANES) * LANES
    levels = state.shape[0]
    whole = pl.BlockSpec(memory_space=pltpu.VMEM)
    there = pl.BlockSpec(memory_space=pl.ANY)
    held = pltpu.VMEM((SECOND - FIRST, levels, WIDTH), BF16)
    return pl.pallas_call(
        outgoing_kernel,
        out_shape=(
            jax.ShapeDtypeStruct((slots, width), BF16),
            jax.ShapeDtypeStruct((slots // LANES, LANES), F32),
            jax.ShapeDtypeStruct((1, padded), F32),
            pltpu.HBM(swept.shape, BF16),
        ),
        in_specs=[pl.BlockSpec(memory_space=pltpu.SMEM)] + [whole] * 6 + [there] * 4,
        out_specs=(whole, whole, whole, there),
        input_output_aliases={10: 3},
        scratch_shapes=[
            pltpu.VMEM((slots, width), F32),
            pltpu.VMEM((LANES, 8 * LANES), BF16),
            pltpu.VMEM((MANY * LANES, 16 * LANES), F32),
            pltpu.VMEM(weights.shape, BF16),
            held,
            held,
            held,
            pltpu.SemaphoreType.DMA((lists // GROUP,)),
            pltpu.SemaphoreType.DMA((3, SECOND - FIRST)),
        ],
        compiler_params=pltpu.CompilerParams(vmem_limit_bytes=32 << 20),
        name="outgoing",
    )(section, atmos, length, ids, owned, blocks, ops, weights, state, coef, swept)


def early_kernel(ops_ref, state_ref, coef_ref, swept_hbm, out_ref):
    out_ref[...] = advance(ops_ref, state_ref[...], coef_ref[...])


def early_sweep(ops, state, coef, swept, start, stop):
    levels, _ = state.shape
    columns = pl.BlockSpec((levels, WIDTH), lambda i: (0, early_column(i + start)))
    there = pl.BlockSpec(memory_space=pl.ANY)
    return pl.pallas_call(
        early_kernel,
        grid=(stop - start,),
        out_shape=pltpu.HBM(swept.shape, BF16),
        in_specs=[pl.BlockSpec(ops.shape, lambda i: (0, 0, 0)), columns, columns, there],
        out_specs=pl.BlockSpec((levels, WIDTH), lambda i: (0, i + start)),
        input_output_aliases={3: 0},
        compiler_params=pltpu.CompilerParams(vmem_limit_bytes=16 << 20),
        name="early",
    )(ops, state, coef, swept)


def backward_lists(arrived_ref, weights_hbm, weights, terms, spread, wide, weight_sems):
    left = lanes_below((8, LANES), BLK)
    mine = own_slot(8, 2 * LANES)
    fill_spread(spread)

    def lists(part, carry):
        for piece in range(MANY):
            fetch_weights(weights_hbm, weights, weight_sems, part * MANY + piece).wait()
        for inner in range(MANY * GROUP):
            tile = part * MANY * GROUP + inner
            echoes = arrived_ref[pl.ds(pl.multiple_of(tile * 16, 16), 16), :].astype(F32)
            for half in range(2):
                lines = []
                for duo in range(NF // 2):
                    both = echoes[half * 8 : half * 8 + 8, duo * LANES : (duo + 1) * LANES]
                    turned = pltpu.roll(both, BLK, 1)
                    lines += [
                        jnp.where(left, both, 0.0),
                        jnp.where(left, 0.0, turned),
                        jnp.where(left, turned, 0.0),
                        jnp.where(left, 0.0, both),
                    ]
                product = lax.dot_general(
                    jnp.concatenate(lines, 0).astype(BF16),
                    half_list(weights, tile, half),
                    (((1,), (1,)), ((), ())),
                    preferred_element_type=F32,
                )
                start = inner * 16 + half * 8
                for line in range(2 * NF):
                    wide[start : start + 8, line * 2 * LANES : (line + 1) * 2 * LANES] = jnp.where(
                        mine, product[line * 8 : line * 8 + 8], 0.0
                    )
        span = MANY * LANES
        here = pl.ds(pl.multiple_of(part * span, span), span)
        for duo in range(NF // 2):
            terms[here, duo * LANES : (duo + 1) * LANES] = lax.dot_general(
                wide[:, duo * 8 * LANES : (duo + 1) * 8 * LANES].astype(BF16),
                spread[...],
                (((1,), (1,)), ((), ())),
                preferred_element_type=F32,
            ).astype(BF16)
        return carry

    lax.fori_loop(0, weights.shape[0] // GROUP // MANY, lists, 0)


def sum_terms(key_ref, table_ref, terms, forcing):
    slots = terms.shape[0]
    pairs = forcing.shape[0] // 8
    table = jnp.broadcast_to(table_ref[...], (LANES, table_ref.shape[1])).T[: 2 * pairs]
    picks = [
        jnp.where(table == key_ref[r : r + 1, :], 1.0, 0.0).astype(BF16)
        for r in range(slots // LANES)
    ]
    total = jnp.dot(jnp.concatenate(picks, 1), terms[...], preferred_element_type=F32)
    left = lanes_below((pairs, LANES), BLK)
    for duo in range(NF // 2):
        even = total[:pairs, duo * LANES : (duo + 1) * LANES]
        odd = total[pairs:, duo * LANES : (duo + 1) * LANES]
        fields = (
            jnp.where(left, even, pltpu.roll(odd, BLK, 1)),
            jnp.where(left, pltpu.roll(even, BLK, 1), odd),
        )
        for n, field in enumerate(fields):
            coarse = field.astype(BF16).astype(F32)
            forcing[pl.ds(2 * duo + n, pairs, stride=8), :] = coarse
            forcing[pl.ds(NF + 2 * duo + n, pairs, stride=8), :] = field - coarse


def late_kernel(
    section_ref,
    key_ref,
    table_ref,
    arrived_hbm,
    weights_hbm,
    write_ref,
    ops_ref,
    swept_hbm,
    state_ref,
    coef_ref,
    out_hbm,
    arrived,
    terms,
    forcing,
    early,
    last,
    spread,
    wide,
    weights,
    weight_sems,
    sems,
):
    step = pl.program_id(0)
    backward = jnp.logical_and(step == 0, section_ref[0] == 0)
    slot = step % 2
    before = 1 - slot
    arrival = pltpu.make_async_copy(arrived_hbm, arrived, sems.at[6])

    def fetch(block, into):
        columns = pl.ds(pl.multiple_of(block * 2 * WIDTH, 2 * WIDTH), 2 * WIDTH)
        return pltpu.make_async_copy(swept_hbm.at[:, columns], early.at[into], sems.at[4 + into])

    @pl.when(step == 0)
    def _():
        arrival.start()
        fetch(step, slot).start()

    @pl.when(backward)
    def _():
        for part in range(weight_sems.shape[0]):
            fetch_weights(weights_hbm, weights, weight_sems, part).start()

    span = 3 * WIDTH
    ready = pltpu.make_async_copy(
        early.at[slot],
        out_hbm.at[:, pl.ds(pl.multiple_of(step * span, span), 2 * WIDTH)],
        sems.at[slot],
    )
    swept = pltpu.make_async_copy(
        last.at[slot],
        out_hbm.at[:, pl.ds(pl.multiple_of(step * span + 2 * WIDTH, WIDTH), WIDTH)],
        sems.at[2 + slot],
    )
    ready_before = pltpu.make_async_copy(
        early.at[before], out_hbm.at[:, pl.ds(0, 2 * WIDTH)], sems.at[before]
    )
    swept_before = pltpu.make_async_copy(
        last.at[before], out_hbm.at[:, pl.ds(0, WIDTH)], sems.at[2 + before]
    )

    last[slot] = advance(ops_ref, state_ref[...], coef_ref[...])

    @pl.when(backward)
    def _():
        arrival.wait()
        backward_lists(arrived, weights_hbm, weights, terms, spread, wide, weight_sems)

    @pl.when(step == 0)
    def _():
        @pl.when(section_ref[0] == 1)
        def _():
            arrival.wait()
            terms[...] = arrived[...]

        sum_terms(key_ref, table_ref, terms, forcing)

    write = write_ref[...]
    coarse = write.astype(BF16).astype(F32)
    fine = write - coarse
    factor = jnp.concatenate([coarse, coarse, fine, fine], 0).astype(BF16)

    def added(start, width):
        base = step * (span // LANES) + start // LANES
        fields = jnp.concatenate(
            [
                forcing[pl.ds(pl.multiple_of((base + t) * 8, 8), 8), :]
                for t in range(width // LANES)
            ],
            1,
        )
        operand = jnp.concatenate([fields, fields], 0).astype(BF16)
        return lax.dot_general(
            factor, operand, (((0,), (0,)), ((), ())), preferred_element_type=F32
        )

    fetch(step, slot).wait()
    early[slot] = (early[slot].astype(F32) + added(0, 2 * WIDTH)).astype(BF16)
    ready.start()
    last[slot] = (last[slot].astype(F32) + added(2 * WIDTH, WIDTH)).astype(BF16)
    swept.start()

    @pl.when(step > 0)
    def _():
        ready_before.wait()
        swept_before.wait()

    @pl.when(step < pl.num_programs(0) - 1)
    def _():
        fetch(step + 1, before).start()

    @pl.when(step == pl.num_programs(0) - 1)
    def _():
        ready.wait()
        swept.wait()


def late(section, key, table, arrived, weights, write, ops, swept, state, coef):
    levels, cells = state.shape
    slots, width = arrived.shape
    whole = pl.BlockSpec(memory_space=pltpu.VMEM)
    columns = pl.BlockSpec((levels, WIDTH), lambda i: (0, 3 * i + 2))
    return pl.pallas_call(
        late_kernel,
        grid=(cells // (3 * WIDTH),),
        out_shape=jax.ShapeDtypeStruct((levels, cells), BF16),
        in_specs=[
            pl.BlockSpec(memory_space=pltpu.SMEM),
            whole,
            whole,
            pl.BlockSpec(memory_space=pl.ANY),
            pl.BlockSpec(memory_space=pl.ANY),
            whole,
            whole,
            pl.BlockSpec(memory_space=pl.ANY),
            columns,
            columns,
        ],
        out_specs=pl.BlockSpec(memory_space=pl.ANY),
        scratch_shapes=[
            pltpu.VMEM((slots, width), BF16),
            pltpu.VMEM((slots, width), BF16),
            pltpu.VMEM((cells // LANES * 8, LANES), F32),
            pltpu.VMEM((2, levels, 2 * WIDTH), BF16),
            pltpu.VMEM((2, levels, WIDTH), BF16),
            pltpu.VMEM((LANES, 8 * LANES), BF16),
            pltpu.VMEM((MANY * LANES, 16 * LANES), F32),
            pltpu.VMEM(weights.shape, BF16),
            pltpu.SemaphoreType.DMA((weights.shape[0] // GROUP,)),
            pltpu.SemaphoreType.DMA((7,)),
        ],
        compiler_params=pltpu.CompilerParams(vmem_limit_bytes=36 << 20),
        name="late",
    )(section, key, table, arrived, weights, write, ops, swept, state, coef)


def body(
    adjoint_state,
    tangent_coef,
    column_ops,
    surf_read,
    surf_write,
    remap_weights,
    pair_atmos,
    pair_ocean,
    list_len,
    ocean_owned,
):
    section = lax.axis_index("sec")
    lists, cap = pair_atmos.shape[1:]
    state = pltpu.with_memory_space_constraint(adjoint_state[0], pltpu.HBM)
    coef = pltpu.with_memory_space_constraint(tangent_coef[0], pltpu.HBM)
    weights = pltpu.with_memory_space_constraint(
        remap_weights[0].reshape(lists, cap // 8, 8, BLK * BLK), pltpu.HBM
    )
    ops = column_ops[0]
    which = section.reshape(1).astype(jnp.int32)
    arrived_ids = lax.all_to_all(pair_ocean[0], "tile", split_axis=0, concat_axis=0, tiled=True)
    read = pltpu.with_memory_space_constraint(surf_read[0], pltpu.HBM)
    surface, swept = surface_blocks(read, ops, state, coef)
    partner = lax.ppermute(surface, "sec", [(0, 1), (1, 0)])
    payload, in_key, in_table, swept = outgoing(
        which,
        pair_atmos[0].T,
        list_len,
        arrived_ids.reshape(lists, 1, cap),
        ocean_owned,
        partner,
        ops,
        weights,
        state,
        coef,
        swept,
    )
    received = lax.all_to_all(
        payload.reshape(lists, cap, NF * BLK), "tile", split_axis=0, concat_axis=0, tiled=True
    )
    swept = early_sweep(ops, state, coef, swept, SECOND, 6)
    swept = pltpu.with_memory_space_constraint(swept, pltpu.HBM)
    arrived = received.reshape(lists * cap, NF * BLK)
    write = surf_write[0].T
    out = late(which, in_key, in_table, arrived, weights, write, ops, swept, state, coef)
    return out[None]


def solution(mesh):
    in_specs = (
        P("sec", None, "tile"),
        P("sec", None, "tile"),
        P("sec", None, None, None),
        P("sec", None, None),
        P("sec", None, None),
        P("tile", None, None, None),
        P("tile", None, None),
        P("tile", None, None),
        P("tile", None),
        P("tile", None),
    )
    out_specs = P("sec", None, "tile")
    return jax.shard_map(body, mesh=mesh, in_specs=in_specs, out_specs=out_specs, check_vma=False)
```

```python
import jax
import jax.numpy as jnp
from jax import lax
from jax.experimental import pallas as pl
from jax.experimental.pallas import tpu as pltpu
from jax.sharding import PartitionSpec as P

NF = 4
BLK = 64
NSTEP = 16
LANES = 128
GROUP = 8
MANY = 2
WIDTH = 4096
FIRST = 2
BF16 = jnp.bfloat16
F32 = jnp.float32


def lanes_below(shape, edge):
    return lax.broadcasted_iota(jnp.int32, shape, len(shape) - 1) < edge


def advance(ops_ref, current, coef):
    factors = coef.astype(F32)
    for step in range(NSTEP):
        stepped = lax.dot_general(
            ops_ref[step], current, (((0,), (0,)), ((), ())), preferred_element_type=F32
        )
        current = (stepped * factors).astype(BF16)
    return current


def early_column(block):
    return block // 2 * 3 + block % 2


def surface_kernel(
    read_ref, ops_ref, state_hbm, coef_hbm, out_ref, swept_hbm, state, coef, swept, held, sems
):
    count = coef.shape[0]
    parts = sems.shape[0] - 2 * count
    tiles = WIDTH // LANES

    def columns(part):
        return pl.ds(pl.multiple_of(part * WIDTH, WIDTH), WIDTH)

    def fetch(part):
        return pltpu.make_async_copy(
            state_hbm.at[:, columns(part)], state.at[:, columns(part)], sems.at[part]
        )

    def fetch_coef(block):
        return pltpu.make_async_copy(
            coef_hbm.at[:, columns(early_column(block))], coef.at[block], sems.at[parts + block]
        )

    def store(block):
        return pltpu.make_async_copy(
            swept.at[block], swept_hbm.at[:, columns(block)], sems.at[parts + count + block]
        )

    ahead = [early_column(block) for block in range(count)]
    for block in range(count):
        fetch(ahead[block]).start()
        fetch_coef(block).start()
    for part in range(parts):
        if part not in ahead:
            fetch(part).start()

    def sweep_block(block, carry):
        part = early_column(block)
        fetch(part).wait()
        fetch_coef(block).wait()
        swept[block] = advance(ops_ref, state[:, columns(part)], coef[block])
        store(block).start()
        return carry

    lax.fori_loop(0, count, sweep_block, 0)
    for part in range(parts):
        if part not in ahead:
            fetch(part).wait()

    def compute(part, carry):
        fields = jnp.dot(read_ref[...], state[:, columns(part)], preferred_element_type=F32)
        for tile in range(tiles):
            row = pl.multiple_of((part * tiles + tile) * 8, 8)
            held[pl.ds(row, NF), :] = fields[:, tile * LANES : (tile + 1) * LANES]
        return carry

    lax.fori_loop(0, parts, compute, 0)
    pairs = out_ref.shape[0] // 2
    left = lanes_below((pairs, LANES), BLK)
    for duo in range(NF // 2):
        first = held[pl.ds(2 * duo, pairs, stride=8), :]
        second = held[pl.ds(2 * duo + 1, pairs, stride=8), :]
        cols = slice(duo * LANES, (duo + 1) * LANES)
        even = jnp.where(left, first, pltpu.roll(second, BLK, 1))
        odd = jnp.where(left, pltpu.roll(first, BLK, 1), second)
        out_ref[:pairs, cols] = even.astype(BF16)
        out_ref[pairs:, cols] = odd.astype(BF16)
    for block in range(count):
        store(block).wait()


def surface_blocks(read, ops, state, coef):
    levels, cells = state.shape
    blocks = cells // BLK
    parts = cells // WIDTH
    whole = pl.BlockSpec(memory_space=pltpu.VMEM)
    there = pl.BlockSpec(memory_space=pl.ANY)
    return pl.pallas_call(
        surface_kernel,
        out_shape=(
            jax.ShapeDtypeStruct((blocks, NF * BLK), BF16),
            pltpu.HBM((levels, cells // 3 * 2), BF16),
        ),
        in_specs=[whole, whole, there, there],
        out_specs=(whole, there),
        scratch_shapes=[
            pltpu.VMEM((levels, cells), BF16),
            pltpu.VMEM((FIRST, levels, WIDTH), BF16),
            pltpu.VMEM((FIRST, levels, WIDTH), BF16),
            pltpu.VMEM((blocks // 2 * 8, LANES), F32),
            pltpu.SemaphoreType.DMA((parts + 2 * FIRST,)),
        ],
        compiler_params=pltpu.CompilerParams(vmem_limit_bytes=28 << 20),
        name="surface",
    )(read, ops, state, coef)


def fetch_weights(weights_hbm, weights, sems, part):
    lists = pl.ds(part * GROUP, GROUP)
    return pltpu.make_async_copy(weights_hbm.at[lists], weights.at[lists], sems.at[part])


def half_list(weights, tile, half):
    return jnp.concatenate(
        [weights[tile, half, :, q * LANES : (q + 1) * LANES] for q in range(BLK // 2)], 0
    )


def fill_spread(spread):
    row = lax.broadcasted_iota(jnp.int32, spread.shape, 0)
    col = lax.broadcasted_iota(jnp.int32, spread.shape, 1)
    source = (col >> 9) * BLK + ((col >> 3) & 31) * 2 + ((col >> 8) & 1)
    spread[...] = jnp.where(row == source, 1.0, 0.0).astype(BF16)


def own_slot(rows, cols):
    row = lax.broadcasted_iota(jnp.int32, (rows, cols), 0)
    col = lax.broadcasted_iota(jnp.int32, (rows, cols), 1)
    return (row & 7) == (col & 7)


def pick(values, lanes):
    return jnp.take_along_axis(values, lanes, axis=1, mode="promise_in_bounds")


def widened(values):
    rows, cols = values.shape
    return jnp.concatenate([values, jnp.zeros((rows, LANES - cols), values.dtype)], 1)


def slot_rows(values):
    lists = values.shape[0]
    lane = lax.broadcasted_iota(jnp.int32, (lists, LANES), 1)
    row = lax.broadcasted_iota(jnp.int32, (lists, LANES), 0)
    spread = jnp.where((lane >> 4) == (row & 7), pick(widened(values), lane & 15), 0.0)
    return jnp.sum(spread.reshape(lists // 8, 8, LANES), 1)


def even_first(values, padded):
    count = values.shape[1]
    pairs = count // 2
    lane = lax.broadcasted_iota(jnp.int32, (8, LANES), 1)
    sources = []
    for start in range(0, count, LANES):
        source = values[:, start : min(start + LANES, count)]
        sources.append(source if source.shape[1] == LANES else widened(source))
    sources = [jnp.broadcast_to(source, (8, LANES)) for source in sources]
    tiles = []
    for tile in range(padded // LANES):
        spots = [
            2 * j if j < pairs else 2 * (j - pairs) + 1
            for j in range(tile * LANES, min((tile + 1) * LANES, count))
        ]
        at = tile * LANES + lane
        wanted = jnp.where(at < pairs, 2 * at, 2 * (at - pairs) + 1)
        result = jnp.full((8, LANES), -2.0, F32)
        for index in sorted({spot // LANES for spot in spots}):
            inside = ((wanted >> 7) == index) & (at < count)
            result = jnp.where(inside, pick(sources[index], wanted & 127), result)
        tiles.append(result)
    return jnp.concatenate(tiles, 1)[:1]


def outgoing_kernel(
    section_ref,
    atmos_ref,
    length_ref,
    ids_ref,
    owned_ref,
    blocks_ref,
    weights_hbm,
    out_ref,
    in_key_ref,
    in_table_ref,
    chosen,
    spread,
    wide,
    weights,
    weight_sems,
):
    @pl.when(section_ref[0] == 1)
    def _():
        for part in range(weight_sems.shape[0]):
            fetch_weights(weights_hbm, weights, weight_sems, part).start()

    blocks = blocks_ref.shape[0]
    pairs = blocks // 2
    padded = in_table_ref.shape[1]
    parts = in_key_ref.shape[0]
    first = section_ref[0] == 0
    lane = lax.broadcasted_iota(jnp.int32, (8, LANES), 1)
    row = lax.broadcasted_iota(jnp.int32, (8, LANES), 0)
    lengths = jnp.broadcast_to(widened(length_ref[...].astype(F32)), (8, LANES))
    live = (lane & 15).astype(F32) < pick(lengths, row * 8 + (lane >> 4))
    atmos = atmos_ref[...]
    atmos = ((atmos & 1) * pairs + (atmos >> 1)).astype(F32)
    atmos_key = jnp.where(live, slot_rows(widened(atmos).T[: atmos.shape[1]]), -1.0)
    ocean_key = slot_rows(ids_ref[:, 0, :].astype(F32))
    owned_table = even_first(owned_ref[...].astype(F32), padded)
    plain_table = lax.broadcasted_iota(jnp.int32, (1, padded), 1).astype(F32)
    out_key = jnp.where(first, ocean_key, atmos_key)
    out_table = jnp.where(first, owned_table, plain_table)
    in_key_ref[...] = jnp.where(first, atmos_key, ocean_key)
    in_table_ref[...] = jnp.where(first, plain_table, owned_table)

    for part in range(parts):
        key = jnp.broadcast_to(out_key[part : part + 1, :], (LANES, LANES)).T
        pieces = []
        for start in range(0, blocks, LANES):
            stop = min(start + LANES, blocks)
            piece = jnp.where(key == out_table[:, start : start + LANES], 1.0, 0.0).astype(BF16)
            pieces.append(piece[:, : stop - start])
        chosen[part * LANES : (part + 1) * LANES, :] = jnp.dot(
            jnp.concatenate(pieces, 1), blocks_ref[...], preferred_element_type=F32
        )

    @pl.when(first)
    def _():
        out_ref[...] = chosen[...].astype(BF16)

    @pl.when(jnp.logical_not(first))
    def _():
        fill_spread(spread)
        left = lane < BLK
        mine = own_slot(MANY * LANES, 2 * LANES)

        def lists(part, carry):
            span = MANY * LANES
            here = pl.ds(pl.multiple_of(part * span, span), span)
            for duo in range(NF // 2):
                values = chosen[here, duo * LANES : (duo + 1) * LANES].astype(BF16)
                for chunk in range(4):
                    cols = slice(chunk * 2 * LANES, (chunk + 1) * 2 * LANES)
                    spaced = jnp.dot(values, spread[:, cols], preferred_element_type=F32)
                    wide[:, (duo * 4 + chunk) * 2 * LANES : (duo * 4 + chunk + 1) * 2 * LANES] = (
                        jnp.where(mine, spaced, 0.0)
                    )
            for piece in range(MANY):
                fetch_weights(weights_hbm, weights, weight_sems, part * MANY + piece).wait()
            for inner in range(MANY * GROUP):
                tile = part * MANY * GROUP + inner
                rows = pl.ds(pl.multiple_of(tile * 16, 16), 16)
                results = []
                for half in range(2):
                    start = inner * 16 + half * 8
                    lines = [
                        wide[start : start + 8, line * 2 * LANES : (line + 1) * 2 * LANES]
                        for line in range(2 * NF)
                    ]
                    product = jnp.dot(
                        jnp.concatenate(lines, 0).astype(BF16),
                        half_list(weights, tile, half),
                        preferred_element_type=F32,
                    )
                    sums = []
                    for field in range(NF):
                        even = product[field * 16 : field * 16 + 8]
                        odd = product[field * 16 + 8 : field * 16 + 16]
                        total = jnp.where(left, even, odd)
                        sums.append(total + pltpu.roll(total, BLK, 1))
                    results.append(
                        [jnp.where(left, sums[2 * duo], sums[2 * duo + 1]) for duo in range(NF // 2)]
                    )
                for duo in range(NF // 2):
                    out_ref[rows, duo * LANES : (duo + 1) * LANES] = jnp.concatenate(
                        [results[0][duo], results[1][duo]], 0
                    ).astype(BF16)
            return carry

        lax.fori_loop(0, parts // MANY, lists, 0)


def outgoing(section, atmos, length, ids, owned, blocks, weights):
    lists, halves, cap, _ = weights.shape
    slots = lists * halves * cap
    count, width = blocks.shape
    padded = -(-count // LANES) * LANES
    whole = pl.BlockSpec(memory_space=pltpu.VMEM)
    there = pl.BlockSpec(memory_space=pl.ANY)
    return pl.pallas_call(
        outgoing_kernel,
        out_shape=(
            jax.ShapeDtypeStruct((slots, width), BF16),
            jax.ShapeDtypeStruct((slots // LANES, LANES), F32),
            jax.ShapeDtypeStruct((1, padded), F32),
        ),
        in_specs=[pl.BlockSpec(memory_space=pltpu.SMEM)] + [whole] * 5 + [there],
        out_specs=(whole,) * 3,
        scratch_shapes=[
            pltpu.VMEM((slots, width), F32),
            pltpu.VMEM((LANES, 8 * LANES), BF16),
            pltpu.VMEM((MANY * LANES, 16 * LANES), F32),
            pltpu.VMEM(weights.shape, BF16),
            pltpu.SemaphoreType.DMA((lists // GROUP,)),
        ],
        compiler_params=pltpu.CompilerParams(vmem_limit_bytes=32 << 20),
        name="outgoing",
    )(section, atmos, length, ids, owned, blocks, weights)


def early_kernel(ops_ref, state_ref, coef_ref, swept_hbm, out_ref):
    out_ref[...] = advance(ops_ref, state_ref[...], coef_ref[...])


def early_sweep(ops, state, coef, swept, start, stop):
    levels, _ = state.shape
    columns = pl.BlockSpec((levels, WIDTH), lambda i: (0, early_column(i + start)))
    there = pl.BlockSpec(memory_space=pl.ANY)
    return pl.pallas_call(
        early_kernel,
        grid=(stop - start,),
        out_shape=pltpu.HBM(swept.shape, BF16),
        in_specs=[pl.BlockSpec(ops.shape, lambda i: (0, 0, 0)), columns, columns, there],
        out_specs=pl.BlockSpec((levels, WIDTH), lambda i: (0, i + start)),
        input_output_aliases={3: 0},
        compiler_params=pltpu.CompilerParams(vmem_limit_bytes=16 << 20),
        name="early",
    )(ops, state, coef, swept)


def backward_lists(arrived_ref, weights_hbm, weights, terms, spread, wide, weight_sems):
    left = lanes_below((8, LANES), BLK)
    mine = own_slot(8, 2 * LANES)
    fill_spread(spread)

    def lists(part, carry):
        for piece in range(MANY):
            fetch_weights(weights_hbm, weights, weight_sems, part * MANY + piece).wait()
        for inner in range(MANY * GROUP):
            tile = part * MANY * GROUP + inner
            echoes = arrived_ref[pl.ds(pl.multiple_of(tile * 16, 16), 16), :].astype(F32)
            for half in range(2):
                lines = []
                for duo in range(NF // 2):
                    both = echoes[half * 8 : half * 8 + 8, duo * LANES : (duo + 1) * LANES]
                    turned = pltpu.roll(both, BLK, 1)
                    lines += [
                        jnp.where(left, both, 0.0),
                        jnp.where(left, 0.0, turned),
                        jnp.where(left, turned, 0.0),
                        jnp.where(left, 0.0, both),
                    ]
                product = lax.dot_general(
                    jnp.concatenate(lines, 0).astype(BF16),
                    half_list(weights, tile, half),
                    (((1,), (1,)), ((), ())),
                    preferred_element_type=F32,
                )
                start = inner * 16 + half * 8
                for line in range(2 * NF):
                    wide[start : start + 8, line * 2 * LANES : (line + 1) * 2 * LANES] = jnp.where(
                        mine, product[line * 8 : line * 8 + 8], 0.0
                    )
        span = MANY * LANES
        here = pl.ds(pl.multiple_of(part * span, span), span)
        for duo in range(NF // 2):
            terms[here, duo * LANES : (duo + 1) * LANES] = lax.dot_general(
                wide[:, duo * 8 * LANES : (duo + 1) * 8 * LANES].astype(BF16),
                spread[...],
                (((1,), (1,)), ((), ())),
                preferred_element_type=F32,
            ).astype(BF16)
        return carry

    lax.fori_loop(0, weights.shape[0] // GROUP // MANY, lists, 0)


def sum_terms(key_ref, table_ref, terms, forcing):
    slots = terms.shape[0]
    pairs = forcing.shape[0] // 8
    table = jnp.broadcast_to(table_ref[...], (LANES, table_ref.shape[1])).T[: 2 * pairs]
    picks = [
        jnp.where(table == key_ref[r : r + 1, :], 1.0, 0.0).astype(BF16)
        for r in range(slots // LANES)
    ]
    total = jnp.dot(jnp.concatenate(picks, 1), terms[...], preferred_element_type=F32)
    left = lanes_below((pairs, LANES), BLK)
    for duo in range(NF // 2):
        even = total[:pairs, duo * LANES : (duo + 1) * LANES]
        odd = total[pairs:, duo * LANES : (duo + 1) * LANES]
        fields = (
            jnp.where(left, even, pltpu.roll(odd, BLK, 1)),
            jnp.where(left, pltpu.roll(even, BLK, 1), odd),
        )
        for n, field in enumerate(fields):
            coarse = field.astype(BF16).astype(F32)
            forcing[pl.ds(2 * duo + n, pairs, stride=8), :] = coarse
            forcing[pl.ds(NF + 2 * duo + n, pairs, stride=8), :] = field - coarse


def late_kernel(
    section_ref,
    key_ref,
    table_ref,
    arrived_hbm,
    weights_hbm,
    write_ref,
    ops_ref,
    swept_hbm,
    state_ref,
    coef_ref,
    out_hbm,
    arrived,
    terms,
    forcing,
    early,
    last,
    spread,
    wide,
    weights,
    weight_sems,
    sems,
):
    step = pl.program_id(0)
    backward = jnp.logical_and(step == 0, section_ref[0] == 0)
    slot = step % 2
    before = 1 - slot
    arrival = pltpu.make_async_copy(arrived_hbm, arrived, sems.at[6])

    def fetch(block, into):
        columns = pl.ds(pl.multiple_of(block * 2 * WIDTH, 2 * WIDTH), 2 * WIDTH)
        return pltpu.make_async_copy(swept_hbm.at[:, columns], early.at[into], sems.at[4 + into])

    @pl.when(step == 0)
    def _():
        arrival.start()
        fetch(step, slot).start()

    @pl.when(backward)
    def _():
        for part in range(weight_sems.shape[0]):
            fetch_weights(weights_hbm, weights, weight_sems, part).start()

    span = 3 * WIDTH
    ready = pltpu.make_async_copy(
        early.at[slot],
        out_hbm.at[:, pl.ds(pl.multiple_of(step * span, span), 2 * WIDTH)],
        sems.at[slot],
    )
    swept = pltpu.make_async_copy(
        last.at[slot],
        out_hbm.at[:, pl.ds(pl.multiple_of(step * span + 2 * WIDTH, WIDTH), WIDTH)],
        sems.at[2 + slot],
    )
    ready_before = pltpu.make_async_copy(
        early.at[before], out_hbm.at[:, pl.ds(0, 2 * WIDTH)], sems.at[before]
    )
    swept_before = pltpu.make_async_copy(
        last.at[before], out_hbm.at[:, pl.ds(0, WIDTH)], sems.at[2 + before]
    )

    last[slot] = advance(ops_ref, state_ref[...], coef_ref[...])

    @pl.when(backward)
    def _():
        arrival.wait()
        backward_lists(arrived, weights_hbm, weights, terms, spread, wide, weight_sems)

    @pl.when(step == 0)
    def _():
        @pl.when(section_ref[0] == 1)
        def _():
            arrival.wait()
            terms[...] = arrived[...]

        sum_terms(key_ref, table_ref, terms, forcing)

    write = write_ref[...]
    coarse = write.astype(BF16).astype(F32)
    fine = write - coarse
    factor = jnp.concatenate([coarse, coarse, fine, fine], 0).astype(BF16)

    def added(start, width):
        base = step * (span // LANES) + start // LANES
        fields = jnp.concatenate(
            [
                forcing[pl.ds(pl.multiple_of((base + t) * 8, 8), 8), :]
                for t in range(width // LANES)
            ],
            1,
        )
        operand = jnp.concatenate([fields, fields], 0).astype(BF16)
        return lax.dot_general(
            factor, operand, (((0,), (0,)), ((), ())), preferred_element_type=F32
        )

    fetch(step, slot).wait()
    early[slot] = (early[slot].astype(F32) + added(0, 2 * WIDTH)).astype(BF16)
    ready.start()
    last[slot] = (last[slot].astype(F32) + added(2 * WIDTH, WIDTH)).astype(BF16)
    swept.start()

    @pl.when(step > 0)
    def _():
        ready_before.wait()
        swept_before.wait()

    @pl.when(step < pl.num_programs(0) - 1)
    def _():
        fetch(step + 1, before).start()

    @pl.when(step == pl.num_programs(0) - 1)
    def _():
        ready.wait()
        swept.wait()


def late(section, key, table, arrived, weights, write, ops, swept, state, coef):
    levels, cells = state.shape
    slots, width = arrived.shape
    whole = pl.BlockSpec(memory_space=pltpu.VMEM)
    columns = pl.BlockSpec((levels, WIDTH), lambda i: (0, 3 * i + 2))
    return pl.pallas_call(
        late_kernel,
        grid=(cells // (3 * WIDTH),),
        out_shape=jax.ShapeDtypeStruct((levels, cells), BF16),
        in_specs=[
            pl.BlockSpec(memory_space=pltpu.SMEM),
            whole,
            whole,
            pl.BlockSpec(memory_space=pl.ANY),
            pl.BlockSpec(memory_space=pl.ANY),
            whole,
            whole,
            pl.BlockSpec(memory_space=pl.ANY),
            columns,
            columns,
        ],
        out_specs=pl.BlockSpec(memory_space=pl.ANY),
        scratch_shapes=[
            pltpu.VMEM((slots, width), BF16),
            pltpu.VMEM((slots, width), BF16),
            pltpu.VMEM((cells // LANES * 8, LANES), F32),
            pltpu.VMEM((2, levels, 2 * WIDTH), BF16),
            pltpu.VMEM((2, levels, WIDTH), BF16),
            pltpu.VMEM((LANES, 8 * LANES), BF16),
            pltpu.VMEM((MANY * LANES, 16 * LANES), F32),
            pltpu.VMEM(weights.shape, BF16),
            pltpu.SemaphoreType.DMA((weights.shape[0] // GROUP,)),
            pltpu.SemaphoreType.DMA((7,)),
        ],
        compiler_params=pltpu.CompilerParams(vmem_limit_bytes=36 << 20),
        name="late",
    )(section, key, table, arrived, weights, write, ops, swept, state, coef)


def body(
    adjoint_state,
    tangent_coef,
    column_ops,
    surf_read,
    surf_write,
    remap_weights,
    pair_atmos,
    pair_ocean,
    list_len,
    ocean_owned,
):
    section = lax.axis_index("sec")
    lists, cap = pair_atmos.shape[1:]
    state = pltpu.with_memory_space_constraint(adjoint_state[0], pltpu.HBM)
    coef = pltpu.with_memory_space_constraint(tangent_coef[0], pltpu.HBM)
    weights = pltpu.with_memory_space_constraint(
        remap_weights[0].reshape(lists, cap // 8, 8, BLK * BLK), pltpu.HBM
    )
    ops = column_ops[0]
    which = section.reshape(1).astype(jnp.int32)
    arrived_ids = lax.all_to_all(pair_ocean[0], "tile", split_axis=0, concat_axis=0, tiled=True)
    read = pltpu.with_memory_space_constraint(surf_read[0], pltpu.HBM)
    surface, swept = surface_blocks(read, ops, state, coef)
    partner = lax.ppermute(surface, "sec", [(0, 1), (1, 0)])
    payload, in_key, in_table = outgoing(
        which,
        pair_atmos[0].T,
        list_len,
        arrived_ids.reshape(lists, 1, cap),
        ocean_owned,
        partner,
        weights,
    )
    received = lax.all_to_all(
        payload.reshape(lists, cap, NF * BLK), "tile", split_axis=0, concat_axis=0, tiled=True
    )
    swept = early_sweep(ops, state, coef, swept, FIRST, 6)
    swept = pltpu.with_memory_space_constraint(swept, pltpu.HBM)
    arrived = received.reshape(lists * cap, NF * BLK)
    write = surf_write[0].T
    out = late(which, in_key, in_table, arrived, weights, write, ops, swept, state, coef)
    return out[None]


def solution(mesh):
    in_specs = (
        P("sec", None, "tile"),
        P("sec", None, "tile"),
        P("sec", None, None, None),
        P("sec", None, None),
        P("sec", None, None),
        P("tile", None, None, None),
        P("tile", None, None),
        P("tile", None, None),
        P("tile", None),
        P("tile", None),
    )
    out_specs = P("sec", None, "tile")
    return jax.shard_map(body, mesh=mesh, in_specs=in_specs, out_specs=out_specs, check_vma=False)
```

```python
import jax
import jax.numpy as jnp
from jax import lax
from jax.experimental import pallas as pl
from jax.experimental.pallas import tpu as pltpu
from jax.sharding import PartitionSpec as P

NF = 4
BLK = 64
NSTEP = 16
LANES = 128
GROUP = 8
MANY = 2
WIDTH = 4096
FIRST = 2
BF16 = jnp.bfloat16
F32 = jnp.float32


def lanes_below(shape, edge):
    return lax.broadcasted_iota(jnp.int32, shape, len(shape) - 1) < edge


def advance(ops_ref, current, coef):
    factors = coef.astype(F32)
    for step in range(NSTEP):
        stepped = lax.dot_general(
            ops_ref[step], current, (((0,), (0,)), ((), ())), preferred_element_type=F32
        )
        current = (stepped * factors).astype(BF16)
    return current


def early_column(block):
    return block // 2 * 3 + block % 2


def surface_kernel(
    read_ref,
    given_hbm,
    state_hbm,
    coef_hbm,
    out_ref,
    swept_hbm,
    ops_ref,
    given,
    state,
    coef,
    swept,
    held,
    sems,
):
    count = coef.shape[0]
    parts = sems.shape[0] - 2 * count - 1
    operators = pltpu.make_async_copy(given_hbm, given, sems.at[parts + 2 * count])
    operators.start()
    tiles = WIDTH // LANES

    def columns(part):
        return pl.ds(pl.multiple_of(part * WIDTH, WIDTH), WIDTH)

    def fetch(part):
        return pltpu.make_async_copy(
            state_hbm.at[:, columns(part)], state.at[:, columns(part)], sems.at[part]
        )

    def fetch_coef(block):
        return pltpu.make_async_copy(
            coef_hbm.at[:, columns(early_column(block))], coef.at[block], sems.at[parts + block]
        )

    def store(block):
        return pltpu.make_async_copy(
            swept.at[block], swept_hbm.at[:, columns(block)], sems.at[parts + count + block]
        )

    ahead = [early_column(block) for block in range(count)]
    for block in range(count):
        fetch(ahead[block]).start()
        fetch_coef(block).start()
    for part in range(parts):
        if part not in ahead:
            fetch(part).start()

    operators.wait()
    ops_ref[...] = jnp.swapaxes(given[...].astype(F32), 0, 1).astype(BF16)

    def sweep_block(block, carry):
        part = early_column(block)
        fetch(part).wait()
        fetch_coef(block).wait()
        swept[block] = advance(ops_ref, state[:, columns(part)], coef[block])
        store(block).start()
        return carry

    lax.fori_loop(0, count, sweep_block, 0)
    for part in range(parts):
        if part not in ahead:
            fetch(part).wait()

    def compute(part, carry):
        fields = jnp.dot(read_ref[...], state[:, columns(part)], preferred_element_type=F32)
        for tile in range(tiles):
            row = pl.multiple_of((part * tiles + tile) * 8, 8)
            held[pl.ds(row, NF), :] = fields[:, tile * LANES : (tile + 1) * LANES]
        return carry

    lax.fori_loop(0, parts, compute, 0)
    pairs = out_ref.shape[0] // 2
    left = lanes_below((pairs, LANES), BLK)
    for duo in range(NF // 2):
        first = held[pl.ds(2 * duo, pairs, stride=8), :]
        second = held[pl.ds(2 * duo + 1, pairs, stride=8), :]
        cols = slice(duo * LANES, (duo + 1) * LANES)
        even = jnp.where(left, first, pltpu.roll(second, BLK, 1))
        odd = jnp.where(left, pltpu.roll(first, BLK, 1), second)
        out_ref[:pairs, cols] = even.astype(BF16)
        out_ref[pairs:, cols] = odd.astype(BF16)
    for block in range(count):
        store(block).wait()


def surface_blocks(read, given, state, coef):
    levels, cells = state.shape
    blocks = cells // BLK
    parts = cells // WIDTH
    whole = pl.BlockSpec(memory_space=pltpu.VMEM)
    there = pl.BlockSpec(memory_space=pl.ANY)
    return pl.pallas_call(
        surface_kernel,
        out_shape=(
            jax.ShapeDtypeStruct((blocks, NF * BLK), BF16),
            pltpu.HBM((levels, cells // 3 * 2), BF16),
            jax.ShapeDtypeStruct((NSTEP, levels, levels), BF16),
        ),
        in_specs=[whole, there, there, there],
        out_specs=(whole, there, whole),
        scratch_shapes=[
            pltpu.VMEM(given.shape, BF16),
            pltpu.VMEM((levels, cells), BF16),
            pltpu.VMEM((FIRST, levels, WIDTH), BF16),
            pltpu.VMEM((FIRST, levels, WIDTH), BF16),
            pltpu.VMEM((blocks // 2 * 8, LANES), F32),
            pltpu.SemaphoreType.DMA((parts + 2 * FIRST + 1,)),
        ],
        compiler_params=pltpu.CompilerParams(vmem_limit_bytes=28 << 20),
        name="surface",
    )(read, given, state, coef)


def fetch_weights(weights_hbm, weights, sems, part):
    lists = pl.ds(part * GROUP, GROUP)
    return pltpu.make_async_copy(weights_hbm.at[lists], weights.at[lists], sems.at[part])


def half_list(weights, tile, half):
    return jnp.concatenate(
        [weights[tile, half, :, q * LANES : (q + 1) * LANES] for q in range(BLK // 2)], 0
    )


def fill_spread(spread):
    row = lax.broadcasted_iota(jnp.int32, spread.shape, 0)
    col = lax.broadcasted_iota(jnp.int32, spread.shape, 1)
    source = (col >> 9) * BLK + ((col >> 3) & 31) * 2 + ((col >> 8) & 1)
    spread[...] = jnp.where(row == source, 1.0, 0.0).astype(BF16)


def own_slot(rows, cols):
    row = lax.broadcasted_iota(jnp.int32, (rows, cols), 0)
    col = lax.broadcasted_iota(jnp.int32, (rows, cols), 1)
    return (row & 7) == (col & 7)


def pick(values, lanes):
    return jnp.take_along_axis(values, lanes, axis=1, mode="promise_in_bounds")


def widened(values):
    rows, cols = values.shape
    return jnp.concatenate([values, jnp.zeros((rows, LANES - cols), values.dtype)], 1)


def slot_rows(values):
    lists = values.shape[0]
    lane = lax.broadcasted_iota(jnp.int32, (lists, LANES), 1)
    row = lax.broadcasted_iota(jnp.int32, (lists, LANES), 0)
    spread = jnp.where((lane >> 4) == (row & 7), pick(widened(values), lane & 15), 0.0)
    return jnp.sum(spread.reshape(lists // 8, 8, LANES), 1)


def even_first(values, padded):
    count = values.shape[1]
    pairs = count // 2
    lane = lax.broadcasted_iota(jnp.int32, (8, LANES), 1)
    sources = []
    for start in range(0, count, LANES):
        source = values[:, start : min(start + LANES, count)]
        sources.append(source if source.shape[1] == LANES else widened(source))
    sources = [jnp.broadcast_to(source, (8, LANES)) for source in sources]
    tiles = []
    for tile in range(padded // LANES):
        spots = [
            2 * j if j < pairs else 2 * (j - pairs) + 1
            for j in range(tile * LANES, min((tile + 1) * LANES, count))
        ]
        at = tile * LANES + lane
        wanted = jnp.where(at < pairs, 2 * at, 2 * (at - pairs) + 1)
        result = jnp.full((8, LANES), -2.0, F32)
        for index in sorted({spot // LANES for spot in spots}):
            inside = ((wanted >> 7) == index) & (at < count)
            result = jnp.where(inside, pick(sources[index], wanted & 127), result)
        tiles.append(result)
    return jnp.concatenate(tiles, 1)[:1]


def outgoing_kernel(
    section_ref,
    atmos_ref,
    length_ref,
    ids_ref,
    owned_ref,
    blocks_ref,
    weights_hbm,
    out_ref,
    in_key_ref,
    in_table_ref,
    chosen,
    spread,
    wide,
    weights,
    weight_sems,
):
    @pl.when(section_ref[0] == 1)
    def _():
        for part in range(weight_sems.shape[0]):
            fetch_weights(weights_hbm, weights, weight_sems, part).start()

    blocks = blocks_ref.shape[0]
    pairs = blocks // 2
    padded = in_table_ref.shape[1]
    parts = in_key_ref.shape[0]
    first = section_ref[0] == 0
    lane = lax.broadcasted_iota(jnp.int32, (8, LANES), 1)
    row = lax.broadcasted_iota(jnp.int32, (8, LANES), 0)
    lengths = jnp.broadcast_to(widened(length_ref[...].astype(F32)), (8, LANES))
    live = (lane & 15).astype(F32) < pick(lengths, row * 8 + (lane >> 4))
    atmos = atmos_ref[...]
    atmos = ((atmos & 1) * pairs + (atmos >> 1)).astype(F32)
    atmos_key = jnp.where(live, slot_rows(widened(atmos).T[: atmos.shape[1]]), -1.0)
    ocean_key = slot_rows(ids_ref[:, 0, :].astype(F32))
    owned_table = even_first(owned_ref[...].astype(F32), padded)
    plain_table = lax.broadcasted_iota(jnp.int32, (1, padded), 1).astype(F32)
    out_key = jnp.where(first, ocean_key, atmos_key)
    out_table = jnp.where(first, owned_table, plain_table)
    in_key_ref[...] = jnp.where(first, atmos_key, ocean_key)
    in_table_ref[...] = jnp.where(first, plain_table, owned_table)

    for part in range(parts):
        key = jnp.broadcast_to(out_key[part : part + 1, :], (LANES, LANES)).T
        pieces = []
        for start in range(0, blocks, LANES):
            stop = min(start + LANES, blocks)
            piece = jnp.where(key == out_table[:, start : start + LANES], 1.0, 0.0).astype(BF16)
            pieces.append(piece[:, : stop - start])
        chosen[part * LANES : (part + 1) * LANES, :] = jnp.dot(
            jnp.concatenate(pieces, 1), blocks_ref[...], preferred_element_type=F32
        )

    @pl.when(first)
    def _():
        out_ref[...] = chosen[...].astype(BF16)

    @pl.when(jnp.logical_not(first))
    def _():
        fill_spread(spread)
        left = lane < BLK
        mine = own_slot(MANY * LANES, 2 * LANES)

        def lists(part, carry):
            span = MANY * LANES
            here = pl.ds(pl.multiple_of(part * span, span), span)
            for duo in range(NF // 2):
                values = chosen[here, duo * LANES : (duo + 1) * LANES].astype(BF16)
                for chunk in range(4):
                    cols = slice(chunk * 2 * LANES, (chunk + 1) * 2 * LANES)
                    spaced = jnp.dot(values, spread[:, cols], preferred_element_type=F32)
                    wide[:, (duo * 4 + chunk) * 2 * LANES : (duo * 4 + chunk + 1) * 2 * LANES] = (
                        jnp.where(mine, spaced, 0.0)
                    )
            for piece in range(MANY):
                fetch_weights(weights_hbm, weights, weight_sems, part * MANY + piece).wait()
            for inner in range(MANY * GROUP):
                tile = part * MANY * GROUP + inner
                rows = pl.ds(pl.multiple_of(tile * 16, 16), 16)
                results = []
                for half in range(2):
                    start = inner * 16 + half * 8
                    lines = [
                        wide[start : start + 8, line * 2 * LANES : (line + 1) * 2 * LANES]
                        for line in range(2 * NF)
                    ]
                    product = jnp.dot(
                        jnp.concatenate(lines, 0).astype(BF16),
                        half_list(weights, tile, half),
                        preferred_element_type=F32,
                    )
                    sums = []
                    for field in range(NF):
                        even = product[field * 16 : field * 16 + 8]
                        odd = product[field * 16 + 8 : field * 16 + 16]
                        total = jnp.where(left, even, odd)
                        sums.append(total + pltpu.roll(total, BLK, 1))
                    results.append(
                        [jnp.where(left, sums[2 * duo], sums[2 * duo + 1]) for duo in range(NF // 2)]
                    )
                for duo in range(NF // 2):
                    out_ref[rows, duo * LANES : (duo + 1) * LANES] = jnp.concatenate(
                        [results[0][duo], results[1][duo]], 0
                    ).astype(BF16)
            return carry

        lax.fori_loop(0, parts // MANY, lists, 0)


def outgoing(section, atmos, length, ids, owned, blocks, weights):
    lists, halves, cap, _ = weights.shape
    slots = lists * halves * cap
    count, width = blocks.shape
    padded = -(-count // LANES) * LANES
    whole = pl.BlockSpec(memory_space=pltpu.VMEM)
    there = pl.BlockSpec(memory_space=pl.ANY)
    return pl.pallas_call(
        outgoing_kernel,
        out_shape=(
            jax.ShapeDtypeStruct((slots, width), BF16),
            jax.ShapeDtypeStruct((slots // LANES, LANES), F32),
            jax.ShapeDtypeStruct((1, padded), F32),
        ),
        in_specs=[pl.BlockSpec(memory_space=pltpu.SMEM)] + [whole] * 5 + [there],
        out_specs=(whole,) * 3,
        scratch_shapes=[
            pltpu.VMEM((slots, width), F32),
            pltpu.VMEM((LANES, 8 * LANES), BF16),
            pltpu.VMEM((MANY * LANES, 16 * LANES), F32),
            pltpu.VMEM(weights.shape, BF16),
            pltpu.SemaphoreType.DMA((lists // GROUP,)),
        ],
        compiler_params=pltpu.CompilerParams(vmem_limit_bytes=32 << 20),
        name="outgoing",
    )(section, atmos, length, ids, owned, blocks, weights)


def early_kernel(ops_ref, state_ref, coef_ref, swept_hbm, out_ref):
    out_ref[...] = advance(ops_ref, state_ref[...], coef_ref[...])


def early_sweep(ops, state, coef, swept, start, stop):
    levels, _ = state.shape
    columns = pl.BlockSpec((levels, WIDTH), lambda i: (0, early_column(i + start)))
    there = pl.BlockSpec(memory_space=pl.ANY)
    return pl.pallas_call(
        early_kernel,
        grid=(stop - start,),
        out_shape=pltpu.HBM(swept.shape, BF16),
        in_specs=[pl.BlockSpec(ops.shape, lambda i: (0, 0, 0)), columns, columns, there],
        out_specs=pl.BlockSpec((levels, WIDTH), lambda i: (0, i + start)),
        input_output_aliases={3: 0},
        compiler_params=pltpu.CompilerParams(vmem_limit_bytes=16 << 20),
        name="early",
    )(ops, state, coef, swept)


def backward_lists(arrived_ref, weights_hbm, weights, terms, spread, wide, weight_sems):
    left = lanes_below((8, LANES), BLK)
    mine = own_slot(8, 2 * LANES)
    fill_spread(spread)

    def lists(part, carry):
        for piece in range(MANY):
            fetch_weights(weights_hbm, weights, weight_sems, part * MANY + piece).wait()
        for inner in range(MANY * GROUP):
            tile = part * MANY * GROUP + inner
            echoes = arrived_ref[pl.ds(pl.multiple_of(tile * 16, 16), 16), :].astype(F32)
            for half in range(2):
                lines = []
                for duo in range(NF // 2):
                    both = echoes[half * 8 : half * 8 + 8, duo * LANES : (duo + 1) * LANES]
                    turned = pltpu.roll(both, BLK, 1)
                    lines += [
                        jnp.where(left, both, 0.0),
                        jnp.where(left, 0.0, turned),
                        jnp.where(left, turned, 0.0),
                        jnp.where(left, 0.0, both),
                    ]
                product = lax.dot_general(
                    jnp.concatenate(lines, 0).astype(BF16),
                    half_list(weights, tile, half),
                    (((1,), (1,)), ((), ())),
                    preferred_element_type=F32,
                )
                start = inner * 16 + half * 8
                for line in range(2 * NF):
                    wide[start : start + 8, line * 2 * LANES : (line + 1) * 2 * LANES] = jnp.where(
                        mine, product[line * 8 : line * 8 + 8], 0.0
                    )
        span = MANY * LANES
        here = pl.ds(pl.multiple_of(part * span, span), span)
        for duo in range(NF // 2):
            terms[here, duo * LANES : (duo + 1) * LANES] = lax.dot_general(
                wide[:, duo * 8 * LANES : (duo + 1) * 8 * LANES].astype(BF16),
                spread[...],
                (((1,), (1,)), ((), ())),
                preferred_element_type=F32,
            ).astype(BF16)
        return carry

    lax.fori_loop(0, weights.shape[0] // GROUP // MANY, lists, 0)


def sum_terms(key_ref, table_ref, terms, forcing):
    slots = terms.shape[0]
    pairs = forcing.shape[0] // 8
    table = jnp.broadcast_to(table_ref[...], (LANES, table_ref.shape[1])).T[: 2 * pairs]
    picks = [
        jnp.where(table == key_ref[r : r + 1, :], 1.0, 0.0).astype(BF16)
        for r in range(slots // LANES)
    ]
    total = jnp.dot(jnp.concatenate(picks, 1), terms[...], preferred_element_type=F32)
    left = lanes_below((pairs, LANES), BLK)
    for duo in range(NF // 2):
        even = total[:pairs, duo * LANES : (duo + 1) * LANES]
        odd = total[pairs:, duo * LANES : (duo + 1) * LANES]
        fields = (
            jnp.where(left, even, pltpu.roll(odd, BLK, 1)),
            jnp.where(left, pltpu.roll(even, BLK, 1), odd),
        )
        for n, field in enumerate(fields):
            coarse = field.astype(BF16).astype(F32)
            forcing[pl.ds(2 * duo + n, pairs, stride=8), :] = coarse
            forcing[pl.ds(NF + 2 * duo + n, pairs, stride=8), :] = field - coarse


def late_kernel(
    section_ref,
    key_ref,
    table_ref,
    arrived_hbm,
    weights_hbm,
    write_ref,
    ops_ref,
    swept_hbm,
    state_ref,
    coef_ref,
    out_hbm,
    arrived,
    terms,
    forcing,
    early,
    last,
    spread,
    wide,
    weights,
    weight_sems,
    sems,
):
    step = pl.program_id(0)
    backward = jnp.logical_and(step == 0, section_ref[0] == 0)
    slot = step % 2
    before = 1 - slot
    arrival = pltpu.make_async_copy(arrived_hbm, arrived, sems.at[6])

    def fetch(block, into):
        columns = pl.ds(pl.multiple_of(block * 2 * WIDTH, 2 * WIDTH), 2 * WIDTH)
        return pltpu.make_async_copy(swept_hbm.at[:, columns], early.at[into], sems.at[4 + into])

    @pl.when(step == 0)
    def _():
        arrival.start()
        fetch(step, slot).start()

    @pl.when(backward)
    def _():
        for part in range(weight_sems.shape[0]):
            fetch_weights(weights_hbm, weights, weight_sems, part).start()

    span = 3 * WIDTH
    ready = pltpu.make_async_copy(
        early.at[slot],
        out_hbm.at[:, pl.ds(pl.multiple_of(step * span, span), 2 * WIDTH)],
        sems.at[slot],
    )
    swept = pltpu.make_async_copy(
        last.at[slot],
        out_hbm.at[:, pl.ds(pl.multiple_of(step * span + 2 * WIDTH, WIDTH), WIDTH)],
        sems.at[2 + slot],
    )
    ready_before = pltpu.make_async_copy(
        early.at[before], out_hbm.at[:, pl.ds(0, 2 * WIDTH)], sems.at[before]
    )
    swept_before = pltpu.make_async_copy(
        last.at[before], out_hbm.at[:, pl.ds(0, WIDTH)], sems.at[2 + before]
    )

    last[slot] = advance(ops_ref, state_ref[...], coef_ref[...])

    @pl.when(backward)
    def _():
        arrival.wait()
        backward_lists(arrived, weights_hbm, weights, terms, spread, wide, weight_sems)

    @pl.when(step == 0)
    def _():
        @pl.when(section_ref[0] == 1)
        def _():
            arrival.wait()
            terms[...] = arrived[...]

        sum_terms(key_ref, table_ref, terms, forcing)

    write = write_ref[...]
    coarse = write.astype(BF16).astype(F32)
    fine = write - coarse
    factor = jnp.concatenate([coarse, coarse, fine, fine], 0).astype(BF16)

    def added(start, width):
        base = step * (span // LANES) + start // LANES
        fields = jnp.concatenate(
            [
                forcing[pl.ds(pl.multiple_of((base + t) * 8, 8), 8), :]
                for t in range(width // LANES)
            ],
            1,
        )
        operand = jnp.concatenate([fields, fields], 0).astype(BF16)
        return lax.dot_general(
            factor, operand, (((0,), (0,)), ((), ())), preferred_element_type=F32
        )

    fetch(step, slot).wait()
    early[slot] = (early[slot].astype(F32) + added(0, 2 * WIDTH)).astype(BF16)
    ready.start()
    last[slot] = (last[slot].astype(F32) + added(2 * WIDTH, WIDTH)).astype(BF16)
    swept.start()

    @pl.when(step > 0)
    def _():
        ready_before.wait()
        swept_before.wait()

    @pl.when(step < pl.num_programs(0) - 1)
    def _():
        fetch(step + 1, before).start()

    @pl.when(step == pl.num_programs(0) - 1)
    def _():
        ready.wait()
        swept.wait()


def late(section, key, table, arrived, weights, write, ops, swept, state, coef):
    levels, cells = state.shape
    slots, width = arrived.shape
    whole = pl.BlockSpec(memory_space=pltpu.VMEM)
    columns = pl.BlockSpec((levels, WIDTH), lambda i: (0, 3 * i + 2))
    return pl.pallas_call(
        late_kernel,
        grid=(cells // (3 * WIDTH),),
        out_shape=jax.ShapeDtypeStruct((levels, cells), BF16),
        in_specs=[
            pl.BlockSpec(memory_space=pltpu.SMEM),
            whole,
            whole,
            pl.BlockSpec(memory_space=pl.ANY),
            pl.BlockSpec(memory_space=pl.ANY),
            whole,
            whole,
            pl.BlockSpec(memory_space=pl.ANY),
            columns,
            columns,
        ],
        out_specs=pl.BlockSpec(memory_space=pl.ANY),
        scratch_shapes=[
            pltpu.VMEM((slots, width), BF16),
            pltpu.VMEM((slots, width), BF16),
            pltpu.VMEM((cells // LANES * 8, LANES), F32),
            pltpu.VMEM((2, levels, 2 * WIDTH), BF16),
            pltpu.VMEM((2, levels, WIDTH), BF16),
            pltpu.VMEM((LANES, 8 * LANES), BF16),
            pltpu.VMEM((MANY * LANES, 16 * LANES), F32),
            pltpu.VMEM(weights.shape, BF16),
            pltpu.SemaphoreType.DMA((weights.shape[0] // GROUP,)),
            pltpu.SemaphoreType.DMA((7,)),
        ],
        compiler_params=pltpu.CompilerParams(vmem_limit_bytes=36 << 20),
        name="late",
    )(section, key, table, arrived, weights, write, ops, swept, state, coef)


def body(
    adjoint_state,
    tangent_coef,
    column_ops,
    surf_read,
    surf_write,
    remap_weights,
    pair_atmos,
    pair_ocean,
    list_len,
    ocean_owned,
):
    section = lax.axis_index("sec")
    lists, cap = pair_atmos.shape[1:]
    state = pltpu.with_memory_space_constraint(adjoint_state[0], pltpu.HBM)
    coef = pltpu.with_memory_space_constraint(tangent_coef[0], pltpu.HBM)
    weights = pltpu.with_memory_space_constraint(
        remap_weights[0].reshape(lists, cap // 8, 8, BLK * BLK), pltpu.HBM
    )
    given = pltpu.with_memory_space_constraint(column_ops[0].transpose(1, 0, 2), pltpu.HBM)
    which = section.reshape(1).astype(jnp.int32)
    arrived_ids = lax.all_to_all(pair_ocean[0], "tile", split_axis=0, concat_axis=0, tiled=True)
    read = pltpu.with_memory_space_constraint(surf_read[0], pltpu.HBM)
    surface, swept, ops = surface_blocks(read, given, state, coef)
    partner = lax.ppermute(surface, "sec", [(0, 1), (1, 0)])
    payload, in_key, in_table = outgoing(
        which,
        pair_atmos[0].T,
        list_len,
        arrived_ids.reshape(lists, 1, cap),
        ocean_owned,
        partner,
        weights,
    )
    received = lax.all_to_all(
        payload.reshape(lists, cap, NF * BLK), "tile", split_axis=0, concat_axis=0, tiled=True
    )
    swept = early_sweep(ops, state, coef, swept, FIRST, 6)
    swept = pltpu.with_memory_space_constraint(swept, pltpu.HBM)
    arrived = received.reshape(lists * cap, NF * BLK)
    write = surf_write[0].T
    out = late(which, in_key, in_table, arrived, weights, write, ops, swept, state, coef)
    return out[None]


def solution(mesh):
    in_specs = (
        P("sec", None, "tile"),
        P("sec", None, "tile"),
        P("sec", None, None, None),
        P("sec", None, None),
        P("sec", None, None),
        P("tile", None, None, None),
        P("tile", None, None),
        P("tile", None, None),
        P("tile", None),
        P("tile", None),
    )
    out_specs = P("sec", None, "tile")
    return jax.shard_map(body, mesh=mesh, in_specs=in_specs, out_specs=out_specs, check_vma=False)
```

```python
import jax
import jax.numpy as jnp
from jax import lax
from jax.experimental import pallas as pl
from jax.experimental.pallas import tpu as pltpu
from jax.sharding import PartitionSpec as P

NF = 4
BLK = 64
NSTEP = 16
LANES = 128
GROUP = 8
MANY = 4
WIDTH = 4096
FIRST = 2
BF16 = jnp.bfloat16
F32 = jnp.float32


def lanes_below(shape, edge):
    return lax.broadcasted_iota(jnp.int32, shape, len(shape) - 1) < edge


def advance(ops_ref, current, coef):
    factors = coef.astype(F32)
    for step in range(NSTEP):
        stepped = lax.dot_general(
            ops_ref[step], current, (((0,), (0,)), ((), ())), preferred_element_type=F32
        )
        current = (stepped * factors).astype(BF16)
    return current


def early_column(block):
    return block // 2 * 3 + block % 2


def surface_kernel(
    read_hbm,
    given_hbm,
    state_hbm,
    coef_hbm,
    out_ref,
    swept_hbm,
    ops_ref,
    read_ref,
    given,
    state,
    coef,
    swept,
    held,
    sems,
):
    count = coef.shape[0]
    parts = sems.shape[0] - 2 * count - 2
    reading = pltpu.make_async_copy(read_hbm, read_ref, sems.at[parts + 2 * count + 1])
    operators = pltpu.make_async_copy(given_hbm, given, sems.at[parts + 2 * count])
    operators.start()
    reading.start()
    tiles = WIDTH // LANES

    def columns(part):
        return pl.ds(pl.multiple_of(part * WIDTH, WIDTH), WIDTH)

    def fetch(part):
        return pltpu.make_async_copy(
            state_hbm.at[:, columns(part)], state.at[:, columns(part)], sems.at[part]
        )

    def fetch_coef(block):
        return pltpu.make_async_copy(
            coef_hbm.at[:, columns(early_column(block))], coef.at[block], sems.at[parts + block]
        )

    def store(block):
        return pltpu.make_async_copy(
            swept.at[block], swept_hbm.at[:, columns(block)], sems.at[parts + count + block]
        )

    ahead = [early_column(block) for block in range(count)]
    for block in range(count):
        fetch(ahead[block]).start()
        fetch_coef(block).start()
    for part in range(parts):
        if part not in ahead:
            fetch(part).start()

    operators.wait()
    reading.wait()
    ops_ref[...] = jnp.swapaxes(given[...].astype(F32), 0, 1).astype(BF16)

    def sweep_block(block, carry):
        part = early_column(block)
        fetch(part).wait()
        fetch_coef(block).wait()
        swept[block] = advance(ops_ref, state[:, columns(part)], coef[block])
        store(block).start()
        return carry

    lax.fori_loop(0, count, sweep_block, 0)
    for part in range(parts):
        if part not in ahead:
            fetch(part).wait()

    def compute(part, carry):
        fields = jnp.dot(read_ref[...], state[:, columns(part)], preferred_element_type=F32)
        for tile in range(tiles):
            row = pl.multiple_of((part * tiles + tile) * 8, 8)
            held[pl.ds(row, NF), :] = fields[:, tile * LANES : (tile + 1) * LANES]
        return carry

    lax.fori_loop(0, parts, compute, 0)
    pairs = out_ref.shape[0] // 2
    left = lanes_below((pairs, LANES), BLK)
    for duo in range(NF // 2):
        first = held[pl.ds(2 * duo, pairs, stride=8), :]
        second = held[pl.ds(2 * duo + 1, pairs, stride=8), :]
        cols = slice(duo * LANES, (duo + 1) * LANES)
        even = jnp.where(left, first, pltpu.roll(second, BLK, 1))
        odd = jnp.where(left, pltpu.roll(first, BLK, 1), second)
        out_ref[:pairs, cols] = even.astype(BF16)
        out_ref[pairs:, cols] = odd.astype(BF16)
    for block in range(count):
        store(block).wait()


def surface_blocks(read, given, state, coef):
    levels, cells = state.shape
    blocks = cells // BLK
    parts = cells // WIDTH
    whole = pl.BlockSpec(memory_space=pltpu.VMEM)
    there = pl.BlockSpec(memory_space=pl.ANY)
    return pl.pallas_call(
        surface_kernel,
        out_shape=(
            jax.ShapeDtypeStruct((blocks, NF * BLK), BF16),
            pltpu.HBM((levels, cells // 3 * 2), BF16),
            jax.ShapeDtypeStruct((NSTEP, levels, levels), BF16),
        ),
        in_specs=[there] * 4,
        out_specs=(whole, there, whole),
        scratch_shapes=[
            pltpu.VMEM(read.shape, BF16),
            pltpu.VMEM(given.shape, BF16),
            pltpu.VMEM((levels, cells), BF16),
            pltpu.VMEM((FIRST, levels, WIDTH), BF16),
            pltpu.VMEM((FIRST, levels, WIDTH), BF16),
            pltpu.VMEM((blocks // 2 * 8, LANES), F32),
            pltpu.SemaphoreType.DMA((parts + 2 * FIRST + 2,)),
        ],
        compiler_params=pltpu.CompilerParams(vmem_limit_bytes=28 << 20),
        name="surface",
    )(read, given, state, coef)


def fetch_weights(weights_hbm, weights, sems, part):
    lists = pl.ds(part * GROUP, GROUP)
    return pltpu.make_async_copy(weights_hbm.at[lists], weights.at[lists], sems.at[part])


def half_list(weights, tile, half):
    return jnp.concatenate(
        [weights[tile, half, :, q * LANES : (q + 1) * LANES] for q in range(BLK // 2)], 0
    )


def fill_spread(spread):
    row = lax.broadcasted_iota(jnp.int32, spread.shape, 0)
    col = lax.broadcasted_iota(jnp.int32, spread.shape, 1)
    source = (col >> 9) * BLK + ((col >> 3) & 31) * 2 + ((col >> 8) & 1)
    spread[...] = jnp.where(row == source, 1.0, 0.0).astype(BF16)


def own_slot(rows, cols):
    row = lax.broadcasted_iota(jnp.int32, (rows, cols), 0)
    col = lax.broadcasted_iota(jnp.int32, (rows, cols), 1)
    return (row & 7) == (col & 7)


def pick(values, lanes):
    return jnp.take_along_axis(values, lanes, axis=1, mode="promise_in_bounds")


def widened(values):
    rows, cols = values.shape
    return jnp.concatenate([values, jnp.zeros((rows, LANES - cols), values.dtype)], 1)


def slot_rows(values):
    lists = values.shape[0]
    lane = lax.broadcasted_iota(jnp.int32, (lists, LANES), 1)
    row = lax.broadcasted_iota(jnp.int32, (lists, LANES), 0)
    spread = jnp.where((lane >> 4) == (row & 7), pick(widened(values), lane & 15), 0.0)
    return jnp.sum(spread.reshape(lists // 8, 8, LANES), 1)


def even_first(values, padded):
    count = values.shape[1]
    pairs = count // 2
    lane = lax.broadcasted_iota(jnp.int32, (8, LANES), 1)
    sources = []
    for start in range(0, count, LANES):
        source = values[:, start : min(start + LANES, count)]
        sources.append(source if source.shape[1] == LANES else widened(source))
    sources = [jnp.broadcast_to(source, (8, LANES)) for source in sources]
    tiles = []
    for tile in range(padded // LANES):
        spots = [
            2 * j if j < pairs else 2 * (j - pairs) + 1
            for j in range(tile * LANES, min((tile + 1) * LANES, count))
        ]
        at = tile * LANES + lane
        wanted = jnp.where(at < pairs, 2 * at, 2 * (at - pairs) + 1)
        result = jnp.full((8, LANES), -2.0, F32)
        for index in sorted({spot // LANES for spot in spots}):
            inside = ((wanted >> 7) == index) & (at < count)
            result = jnp.where(inside, pick(sources[index], wanted & 127), result)
        tiles.append(result)
    return jnp.concatenate(tiles, 1)[:1]


def outgoing_kernel(
    section_ref,
    atmos_ref,
    length_ref,
    ids_ref,
    owned_ref,
    blocks_ref,
    weights_hbm,
    out_ref,
    in_key_ref,
    in_table_ref,
    chosen,
    spread,
    wide,
    weights,
    weight_sems,
):
    @pl.when(section_ref[0] == 1)
    def _():
        for part in range(weight_sems.shape[0]):
            fetch_weights(weights_hbm, weights, weight_sems, part).start()

    blocks = blocks_ref.shape[0]
    pairs = blocks // 2
    padded = in_table_ref.shape[1]
    parts = in_key_ref.shape[0]
    first = section_ref[0] == 0
    lane = lax.broadcasted_iota(jnp.int32, (8, LANES), 1)
    row = lax.broadcasted_iota(jnp.int32, (8, LANES), 0)
    lengths = jnp.broadcast_to(widened(length_ref[...].astype(F32)), (8, LANES))
    live = (lane & 15).astype(F32) < pick(lengths, row * 8 + (lane >> 4))
    atmos = atmos_ref[...]
    atmos = ((atmos & 1) * pairs + (atmos >> 1)).astype(F32)
    atmos_key = jnp.where(live, slot_rows(widened(atmos).T[: atmos.shape[1]]), -1.0)
    ocean_key = slot_rows(ids_ref[:, 0, :].astype(F32))
    owned_table = even_first(owned_ref[...].astype(F32), padded)
    plain_table = lax.broadcasted_iota(jnp.int32, (1, padded), 1).astype(F32)
    out_key = jnp.where(first, ocean_key, atmos_key)
    out_table = jnp.where(first, owned_table, plain_table)
    in_key_ref[...] = jnp.where(first, atmos_key, ocean_key)
    in_table_ref[...] = jnp.where(first, plain_table, owned_table)

    for part in range(parts):
        key = jnp.broadcast_to(out_key[part : part + 1, :], (LANES, LANES)).T
        pieces = []
        for start in range(0, blocks, LANES):
            stop = min(start + LANES, blocks)
            piece = jnp.where(key == out_table[:, start : start + LANES], 1.0, 0.0).astype(BF16)
            pieces.append(piece[:, : stop - start])
        chosen[part * LANES : (part + 1) * LANES, :] = jnp.dot(
            jnp.concatenate(pieces, 1), blocks_ref[...], preferred_element_type=F32
        )

    @pl.when(first)
    def _():
        out_ref[...] = chosen[...].astype(BF16)

    @pl.when(jnp.logical_not(first))
    def _():
        fill_spread(spread)
        left = lane < BLK
        mine = own_slot(MANY * LANES, 2 * LANES)

        def lists(part, carry):
            span = MANY * LANES
            here = pl.ds(pl.multiple_of(part * span, span), span)
            for duo in range(NF // 2):
                values = chosen[here, duo * LANES : (duo + 1) * LANES].astype(BF16)
                for chunk in range(4):
                    cols = slice(chunk * 2 * LANES, (chunk + 1) * 2 * LANES)
                    spaced = jnp.dot(values, spread[:, cols], preferred_element_type=F32)
                    wide[:, (duo * 4 + chunk) * 2 * LANES : (duo * 4 + chunk + 1) * 2 * LANES] = (
                        jnp.where(mine, spaced, 0.0)
                    )
            for piece in range(MANY):
                fetch_weights(weights_hbm, weights, weight_sems, part * MANY + piece).wait()
            for inner in range(MANY * GROUP):
                tile = part * MANY * GROUP + inner
                rows = pl.ds(pl.multiple_of(tile * 16, 16), 16)
                results = []
                for half in range(2):
                    start = inner * 16 + half * 8
                    lines = [
                        wide[start : start + 8, line * 2 * LANES : (line + 1) * 2 * LANES]
                        for line in range(2 * NF)
                    ]
                    product = jnp.dot(
                        jnp.concatenate(lines, 0).astype(BF16),
                        half_list(weights, tile, half),
                        preferred_element_type=F32,
                    )
                    sums = []
                    for field in range(NF):
                        even = product[field * 16 : field * 16 + 8]
                        odd = product[field * 16 + 8 : field * 16 + 16]
                        total = jnp.where(left, even, odd)
                        sums.append(total + pltpu.roll(total, BLK, 1))
                    results.append(
                        [jnp.where(left, sums[2 * duo], sums[2 * duo + 1]) for duo in range(NF // 2)]
                    )
                for duo in range(NF // 2):
                    out_ref[rows, duo * LANES : (duo + 1) * LANES] = jnp.concatenate(
                        [results[0][duo], results[1][duo]], 0
                    ).astype(BF16)
            return carry

        lax.fori_loop(0, parts // MANY, lists, 0)


def outgoing(section, atmos, length, ids, owned, blocks, weights):
    lists, halves, cap, _ = weights.shape
    slots = lists * halves * cap
    count, width = blocks.shape
    padded = -(-count // LANES) * LANES
    whole = pl.BlockSpec(memory_space=pltpu.VMEM)
    there = pl.BlockSpec(memory_space=pl.ANY)
    return pl.pallas_call(
        outgoing_kernel,
        out_shape=(
            jax.ShapeDtypeStruct((slots, width), BF16),
            jax.ShapeDtypeStruct((slots // LANES, LANES), F32),
            jax.ShapeDtypeStruct((1, padded), F32),
        ),
        in_specs=[pl.BlockSpec(memory_space=pltpu.SMEM)] + [whole] * 5 + [there],
        out_specs=(whole,) * 3,
        scratch_shapes=[
            pltpu.VMEM((slots, width), F32),
            pltpu.VMEM((LANES, 8 * LANES), BF16),
            pltpu.VMEM((MANY * LANES, 16 * LANES), F32),
            pltpu.VMEM(weights.shape, BF16),
            pltpu.SemaphoreType.DMA((lists // GROUP,)),
        ],
        compiler_params=pltpu.CompilerParams(vmem_limit_bytes=32 << 20),
        name="outgoing",
    )(section, atmos, length, ids, owned, blocks, weights)


def early_kernel(ops_ref, state_ref, coef_ref, swept_hbm, out_ref):
    out_ref[...] = advance(ops_ref, state_ref[...], coef_ref[...])


def early_sweep(ops, state, coef, swept, start, stop):
    levels, _ = state.shape
    columns = pl.BlockSpec((levels, WIDTH), lambda i: (0, early_column(i + start)))
    there = pl.BlockSpec(memory_space=pl.ANY)
    return pl.pallas_call(
        early_kernel,
        grid=(stop - start,),
        out_shape=pltpu.HBM(swept.shape, BF16),
        in_specs=[pl.BlockSpec(ops.shape, lambda i: (0, 0, 0)), columns, columns, there],
        out_specs=pl.BlockSpec((levels, WIDTH), lambda i: (0, i + start)),
        input_output_aliases={3: 0},
        compiler_params=pltpu.CompilerParams(vmem_limit_bytes=16 << 20),
        name="early",
    )(ops, state, coef, swept)


def backward_lists(arrived_ref, weights_hbm, weights, terms, spread, wide, weight_sems):
    left = lanes_below((8, LANES), BLK)
    mine = own_slot(8, 2 * LANES)
    fill_spread(spread)

    def lists(part, carry):
        for piece in range(MANY):
            fetch_weights(weights_hbm, weights, weight_sems, part * MANY + piece).wait()
        for inner in range(MANY * GROUP):
            tile = part * MANY * GROUP + inner
            echoes = arrived_ref[pl.ds(pl.multiple_of(tile * 16, 16), 16), :].astype(F32)
            for half in range(2):
                lines = []
                for duo in range(NF // 2):
                    both = echoes[half * 8 : half * 8 + 8, duo * LANES : (duo + 1) * LANES]
                    turned = pltpu.roll(both, BLK, 1)
                    lines += [
                        jnp.where(left, both, 0.0),
                        jnp.where(left, 0.0, turned),
                        jnp.where(left, turned, 0.0),
                        jnp.where(left, 0.0, both),
                    ]
                product = lax.dot_general(
                    jnp.concatenate(lines, 0).astype(BF16),
                    half_list(weights, tile, half),
                    (((1,), (1,)), ((), ())),
                    preferred_element_type=F32,
                )
                start = inner * 16 + half * 8
                for line in range(2 * NF):
                    wide[start : start + 8, line * 2 * LANES : (line + 1) * 2 * LANES] = jnp.where(
                        mine, product[line * 8 : line * 8 + 8], 0.0
                    )
        span = MANY * LANES
        here = pl.ds(pl.multiple_of(part * span, span), span)
        for duo in range(NF // 2):
            terms[here, duo * LANES : (duo + 1) * LANES] = lax.dot_general(
                wide[:, duo * 8 * LANES : (duo + 1) * 8 * LANES].astype(BF16),
                spread[...],
                (((1,), (1,)), ((), ())),
                preferred_element_type=F32,
            ).astype(BF16)
        return carry

    lax.fori_loop(0, weights.shape[0] // GROUP // MANY, lists, 0)


def sum_terms(key_ref, table_ref, terms, forcing):
    slots = terms.shape[0]
    pairs = forcing.shape[0] // 8
    table = jnp.broadcast_to(table_ref[...], (LANES, table_ref.shape[1])).T[: 2 * pairs]
    picks = [
        jnp.where(table == key_ref[r : r + 1, :], 1.0, 0.0).astype(BF16)
        for r in range(slots // LANES)
    ]
    total = jnp.dot(jnp.concatenate(picks, 1), terms[...], preferred_element_type=F32)
    left = lanes_below((pairs, LANES), BLK)
    for duo in range(NF // 2):
        even = total[:pairs, duo * LANES : (duo + 1) * LANES]
        odd = total[pairs:, duo * LANES : (duo + 1) * LANES]
        fields = (
            jnp.where(left, even, pltpu.roll(odd, BLK, 1)),
            jnp.where(left, pltpu.roll(even, BLK, 1), odd),
        )
        for n, field in enumerate(fields):
            coarse = field.astype(BF16).astype(F32)
            forcing[pl.ds(2 * duo + n, pairs, stride=8), :] = coarse
            forcing[pl.ds(NF + 2 * duo + n, pairs, stride=8), :] = field - coarse


def late_kernel(
    section_ref,
    key_ref,
    table_ref,
    arrived_hbm,
    weights_hbm,
    write_ref,
    ops_ref,
    swept_hbm,
    state_ref,
    coef_ref,
    out_hbm,
    arrived,
    terms,
    forcing,
    early,
    last,
    spread,
    wide,
    weights,
    weight_sems,
    sems,
):
    step = pl.program_id(0)
    backward = jnp.logical_and(step == 0, section_ref[0] == 0)
    slot = step % 2
    before = 1 - slot
    arrival = pltpu.make_async_copy(arrived_hbm, arrived, sems.at[6])

    def fetch(block, into):
        columns = pl.ds(pl.multiple_of(block * 2 * WIDTH, 2 * WIDTH), 2 * WIDTH)
        return pltpu.make_async_copy(swept_hbm.at[:, columns], early.at[into], sems.at[4 + into])

    @pl.when(step == 0)
    def _():
        arrival.start()
        fetch(step, slot).start()

    @pl.when(backward)
    def _():
        for part in range(weight_sems.shape[0]):
            fetch_weights(weights_hbm, weights, weight_sems, part).start()

    span = 3 * WIDTH
    ready = pltpu.make_async_copy(
        early.at[slot],
        out_hbm.at[:, pl.ds(pl.multiple_of(step * span, span), 2 * WIDTH)],
        sems.at[slot],
    )
    swept = pltpu.make_async_copy(
        last.at[slot],
        out_hbm.at[:, pl.ds(pl.multiple_of(step * span + 2 * WIDTH, WIDTH), WIDTH)],
        sems.at[2 + slot],
    )
    ready_before = pltpu.make_async_copy(
        early.at[before], out_hbm.at[:, pl.ds(0, 2 * WIDTH)], sems.at[before]
    )
    swept_before = pltpu.make_async_copy(
        last.at[before], out_hbm.at[:, pl.ds(0, WIDTH)], sems.at[2 + before]
    )

    last[slot] = advance(ops_ref, state_ref[...], coef_ref[...])

    @pl.when(backward)
    def _():
        arrival.wait()
        backward_lists(arrived, weights_hbm, weights, terms, spread, wide, weight_sems)

    @pl.when(step == 0)
    def _():
        @pl.when(section_ref[0] == 1)
        def _():
            arrival.wait()
            terms[...] = arrived[...]

        sum_terms(key_ref, table_ref, terms, forcing)

    write = write_ref[...]
    coarse = write.astype(BF16).astype(F32)
    fine = write - coarse
    factor = jnp.concatenate([coarse, coarse, fine, fine], 0).astype(BF16)

    def added(start, width):
        base = step * (span // LANES) + start // LANES
        fields = jnp.concatenate(
            [
                forcing[pl.ds(pl.multiple_of((base + t) * 8, 8), 8), :]
                for t in range(width // LANES)
            ],
            1,
        )
        operand = jnp.concatenate([fields, fields], 0).astype(BF16)
        return lax.dot_general(
            factor, operand, (((0,), (0,)), ((), ())), preferred_element_type=F32
        )

    fetch(step, slot).wait()
    early[slot] = (early[slot].astype(F32) + added(0, 2 * WIDTH)).astype(BF16)
    ready.start()
    last[slot] = (last[slot].astype(F32) + added(2 * WIDTH, WIDTH)).astype(BF16)
    swept.start()

    @pl.when(step > 0)
    def _():
        ready_before.wait()
        swept_before.wait()

    @pl.when(step < pl.num_programs(0) - 1)
    def _():
        fetch(step + 1, before).start()

    @pl.when(step == pl.num_programs(0) - 1)
    def _():
        ready.wait()
        swept.wait()


def late(section, key, table, arrived, weights, write, ops, swept, state, coef):
    levels, cells = state.shape
    slots, width = arrived.shape
    whole = pl.BlockSpec(memory_space=pltpu.VMEM)
    columns = pl.BlockSpec((levels, WIDTH), lambda i: (0, 3 * i + 2))
    return pl.pallas_call(
        late_kernel,
        grid=(cells // (3 * WIDTH),),
        out_shape=jax.ShapeDtypeStruct((levels, cells), BF16),
        in_specs=[
            pl.BlockSpec(memory_space=pltpu.SMEM),
            whole,
            whole,
            pl.BlockSpec(memory_space=pl.ANY),
            pl.BlockSpec(memory_space=pl.ANY),
            whole,
            whole,
            pl.BlockSpec(memory_space=pl.ANY),
            columns,
            columns,
        ],
        out_specs=pl.BlockSpec(memory_space=pl.ANY),
        scratch_shapes=[
            pltpu.VMEM((slots, width), BF16),
            pltpu.VMEM((slots, width), BF16),
            pltpu.VMEM((cells // LANES * 8, LANES), F32),
            pltpu.VMEM((2, levels, 2 * WIDTH), BF16),
            pltpu.VMEM((2, levels, WIDTH), BF16),
            pltpu.VMEM((LANES, 8 * LANES), BF16),
            pltpu.VMEM((MANY * LANES, 16 * LANES), F32),
            pltpu.VMEM(weights.shape, BF16),
            pltpu.SemaphoreType.DMA((weights.shape[0] // GROUP,)),
            pltpu.SemaphoreType.DMA((7,)),
        ],
        compiler_params=pltpu.CompilerParams(vmem_limit_bytes=36 << 20),
        name="late",
    )(section, key, table, arrived, weights, write, ops, swept, state, coef)


def body(
    adjoint_state,
    tangent_coef,
    column_ops,
    surf_read,
    surf_write,
    remap_weights,
    pair_atmos,
    pair_ocean,
    list_len,
    ocean_owned,
):
    section = lax.axis_index("sec")
    lists, cap = pair_atmos.shape[1:]
    state = pltpu.with_memory_space_constraint(adjoint_state[0], pltpu.HBM)
    coef = pltpu.with_memory_space_constraint(tangent_coef[0], pltpu.HBM)
    weights = pltpu.with_memory_space_constraint(
        remap_weights[0].reshape(lists, cap // 8, 8, BLK * BLK), pltpu.HBM
    )
    given = pltpu.with_memory_space_constraint(column_ops[0].transpose(1, 0, 2), pltpu.HBM)
    which = section.reshape(1).astype(jnp.int32)
    arrived_ids = lax.all_to_all(pair_ocean[0], "tile", split_axis=0, concat_axis=0, tiled=True)
    read = pltpu.with_memory_space_constraint(surf_read[0], pltpu.HBM)
    surface, swept, ops = surface_blocks(read, given, state, coef)
    partner = lax.ppermute(surface, "sec", [(0, 1), (1, 0)])
    payload, in_key, in_table = outgoing(
        which,
        pair_atmos[0].T,
        list_len,
        arrived_ids.reshape(lists, 1, cap),
        ocean_owned,
        partner,
        weights,
    )
    received = lax.all_to_all(
        payload.reshape(lists, cap, NF * BLK), "tile", split_axis=0, concat_axis=0, tiled=True
    )
    swept = early_sweep(ops, state, coef, swept, FIRST, 6)
    swept = pltpu.with_memory_space_constraint(swept, pltpu.HBM)
    arrived = received.reshape(lists * cap, NF * BLK)
    write = surf_write[0].T
    out = late(which, in_key, in_table, arrived, weights, write, ops, swept, state, coef)
    return out[None]


def solution(mesh):
    in_specs = (
        P("sec", None, "tile"),
        P("sec", None, "tile"),
        P("sec", None, None, None),
        P("sec", None, None),
        P("sec", None, None),
        P("tile", None, None, None),
        P("tile", None, None),
        P("tile", None, None),
        P("tile", None),
        P("tile", None),
    )
    out_specs = P("sec", None, "tile")
    return jax.shard_map(body, mesh=mesh, in_specs=in_specs, out_specs=out_specs, check_vma=False)
```
